32 devices in a mesh: ctx: 8 (over z, y), wsh: 4 (over x, core).
Axes of the slice: x: 2, y: 2, z: 4, core: 2. Of those that a mesh axis runs over, the one named last changes fastest.
Arguments:
- tokens: bfloat16 [4, 1024, 2048], P('wsh', 'ctx'), may hold values from -6 to 6
- out_grad: bfloat16 [4, 1024, 2048], P('wsh', 'ctx'), may hold values from -6 to 6
- attn_weight: bfloat16 [4, 2048, 2048], P(None, None, 'wsh'), may hold values from -0.125 to 0.125
- mlp_weight: bfloat16 [3, 2048, 8192], P(None, None, 'wsh'), may hold values from -0.125 to 0.125
- norm_gains: bfloat16 [4, 2048], P(None, 'wsh'), may hold values from 0.25 to 1.75
- adapt_model: bfloat16 [11, 64, 2048], P(None, None, 'wsh'), may hold values from -0.125 to 0.125
- adapt_hidden: bfloat16 [3, 64, 8192], P(None, None, 'wsh'), may hold values from -0.0625 to 0.0625
- lengths: int32 [4], replicated, may hold values from 512 to 1024, as said below
- adapter_pick: int32 [4], replicated, may hold values from 0 to 3
- block_order: int32 [4, 16], P('wsh'), may hold values from 0 to 15, as said below
Outputs:
- layer_out: bfloat16 [4, 1024, 2048], P('wsh', 'ctx')
- input_grad: float32 [4, 1024, 2048], P('wsh', 'ctx')
- adapt_model_grad: float32 [11, 64, 2048], P(None, None, 'wsh')
- adapt_hidden_grad: float32 [3, 64, 8192], P(None, None, 'wsh')
The draws below stay inside these ranges and needn't reach their ends.
Inputs may be any that keep to these rules, and one draw needn't show every extreme that they name: `lengths`: some sequence has exactly 1024 valid tokens. Each row of block_order is a permutation of the 16 blocks; the two blocks stored on one index of ctx are p and 15 - p for some p, in either order.
All inputs are finite; a program needn't handle non-finite values.
Results may differ from the reference program's by a relative error of at most 0.017.
Values may be sent and summed in bfloat16 or wider, within the bound.
No kernel may reach another device: no remote copies, remote signals or barrier semaphores. Data moves between devices by JAX's collectives and lax.ppermute only.
A program may use at most 512 MiB of HBM per device.

```python
import math
import jax
import jax.numpy as jnp
from jax import lax

D = 2048
HEADS = 16
HEAD_DIM = 128
FF = 8192
RANK = 16
ADAPTERS = 4
SEQS = 4
SLOT = 1024
BLOCK = 64
BLOCKS = 16


def draw_lengths(key, part):
    first_key, second_key = jax.random.split(key)
    drawn_lengths = jax.random.randint(first_key, (SEQS,), SLOT // 2, SLOT + 1)
    full_at = jax.random.randint(second_key, (), 0, SEQS)
    return jnp.where(jnp.arange(SEQS) == full_at, SLOT, drawn_lengths).astype(jnp.int32)


def draw_block_order(key, part):
    pair_key, flip_key = jax.random.split(key)
    pair_ids = jax.vmap(lambda single: jax.random.permutation(single, BLOCKS // 2))(jax.random.split(pair_key, SEQS))
    flip_bits = jax.random.randint(flip_key, (SEQS, BLOCKS // 2), 0, 2)
    partner = BLOCKS - 1 - pair_ids
    first_block = jnp.where(flip_bits == 1, partner, pair_ids)
    second = jnp.where(flip_bits == 1, pair_ids, partner)
    return jnp.stack([first_block, second], axis=-1).reshape(SEQS, BLOCKS).astype(jnp.int32)


def place_ends(values, stream_key, low, high):
    shape = values.shape
    spot = [jax.random.randint(jax.random.fold_in(stream_key, axis), (), 0, shape[axis]) for axis in range(len(shape))]
    values = values.at[tuple(spot)].set(low)
    longest = shape.index(max(shape))
    spot[longest] = (spot[longest] + 1) % shape[longest]
    return values.at[tuple(spot)].set(high)


def levels(own_key, shape, cuts, smallest, top_value):
    def one(position, blocks):
        steps = jax.random.uniform(jax.random.fold_in(jax.random.fold_in(own_key, 6), position), (blocks,), jnp.float32, smallest / len(cuts), top_value / len(cuts))
        return jnp.repeat(jnp.exp(steps), shape[position] // blocks).reshape((-1,) + (1,) * (len(shape) - position - 1))

    factor_of = one(*cuts[0])
    for cut in cuts[1:]:
        factor_of = factor_of * one(*cut)
    return factor_of


def noise(own_key, extent, deviation, limit, pieces=(), kind=jnp.bfloat16):
    level = levels(own_key, extent, pieces, -0.22, 0.18) if pieces else 1.0
    values = jax.random.normal(own_key, extent, jnp.float32) * deviation * level
    return jnp.minimum(jnp.maximum(values, -limit), limit).astype(kind)


def setup_inputs(seed: int = 0) -> dict:
    arg_keys = jax.random.split(jax.random.key(seed), 11)
    return {
        "tokens": noise(arg_keys[0], (SEQS, SLOT, D), 1.0, 6.0, ((0, 4), (1, 8))),
        "out_grad": noise(arg_keys[1], (SEQS, SLOT, D), 1.0, 6.0, ((0, 4), (1, 8))),
        "attn_weight": noise(arg_keys[2], (4, D, D), D ** -0.5, 0.125, ((2, 4),)),
        "mlp_weight": noise(arg_keys[3], (3, D, FF), D ** -0.5, 0.125, ((2, 4),)),
        "norm_gains": jnp.clip(1.0 + 0.15 * jax.random.normal(arg_keys[4], (4, D), jnp.float32), 0.25, 1.75).astype(jnp.bfloat16),
        "adapt_model": noise(arg_keys[5], (11, ADAPTERS * RANK, D), D ** -0.5, 0.125, ((2, 4),)),
        "adapt_hidden": noise(arg_keys[6], (3, ADAPTERS * RANK, FF), FF ** -0.5, 0.0625, ((2, 4),)),
        "lengths": draw_lengths(jax.random.fold_in(arg_keys[10], 71), 0),
        "adapter_pick": place_ends(jax.random.randint(arg_keys[8], (SEQS,), 0, ADAPTERS), jax.random.fold_in(arg_keys[8], 1), 0, ADAPTERS - 1).astype(jnp.int32),
        "block_order": draw_block_order(jax.random.fold_in(arg_keys[10], 71), 0),
    }


NORM_EPS = 1e-06
ADAPTER_SCALE = 4.0
ROPE_BASE = 500000.0

@jax.custom_vjp
def low(v):
    return lax.optimization_barrier(v.astype(jnp.bfloat16)).astype(jnp.float32)

@jax.custom_vjp
def low_back(v):
    return v

def low_keep(v):
    return (low(v), None)

def low_pass(kept, grad):
    return (grad,)

def back_keep(v):
    return (v, None)

def back_low(kept, grad):
    return (low(grad),)
low.defvjp(low_keep, low_pass)
low_back.defvjp(back_keep, back_low)

def precise_product(left, right):
    return jnp.dot(left, right, precision=lax.Precision.HIGHEST, preferred_element_type=jnp.float32)

def rms_norm(values, gain_row):
    return values * lax.rsqrt(lax.optimization_barrier(jnp.mean(values * values, axis=-1, keepdims=True)) + NORM_EPS) * gain_row

def rotate(values, positions):
    row_count = values.shape[0]
    shaped = values.reshape(row_count, HEADS, HEAD_DIM)
    half_dim = HEAD_DIM // 2
    frequency = ROPE_BASE ** (-(jnp.arange(half_dim, dtype=jnp.float32) * 2.0) / HEAD_DIM)
    angles = positions.astype(jnp.float32)[:, None] * frequency[None, :]
    cosine = jnp.cos(angles)[:, None, :]
    sine_part = jnp.sin(angles)[:, None, :]
    first_half = shaped[..., :half_dim]
    second_half = shaped[..., half_dim:]
    turned = jnp.concatenate([first_half * cosine - second_half * sine_part, second_half * cosine + first_half * sine_part], axis=-1)
    return turned.reshape(row_count, HEADS * HEAD_DIM)

def adapted(input_rows, weight_matrix, down_rows, up_projection_rows):
    reduced_rows = low_back(low(jnp.einsum('td,rd->tr', input_rows, down_rows, precision=lax.Precision.HIGHEST)))
    return precise_product(input_rows, weight_matrix) + ADAPTER_SCALE * precise_product(reduced_rows, up_projection_rows)

def attend(queries, key_rows, values, positions, seq_length):
    row_count = queries.shape[0]
    block_size = math.gcd(512, row_count)
    block_count = row_count // block_size
    shaped_keys = key_rows.reshape(row_count, HEADS, HEAD_DIM)
    shaped_values = values.reshape(row_count, HEADS, HEAD_DIM)

    def one_block(block_items):
        query_block, pos_block = block_items
        scores = jnp.einsum('qhd,khd->hqk', query_block, shaped_keys, precision=lax.Precision.HIGHEST) * HEAD_DIM ** (-0.5)
        scores = low_back(scores)
        allowed = (positions[None, :] <= pos_block[:, None]) & (positions[None, :] < seq_length)
        scores = jnp.where(allowed[None], scores, -jnp.inf)
        weights = low(jnp.exp(scores - jax.nn.logsumexp(scores, axis=-1, keepdims=True)))
        return jnp.einsum('hqk,khd->qhd', weights, shaped_values, precision=lax.Precision.HIGHEST)
    mixed = lax.map(jax.checkpoint(one_block), (queries.reshape(block_count, block_size, HEADS, HEAD_DIM), positions.reshape(block_count, block_size)))
    return mixed.reshape(row_count, HEADS * HEAD_DIM)

def layer_forward(input_rows, model_stack, hidden_stack, onehot, attn_full, mlp_full, gains_all, positions, seq_length):
    model_rows = jnp.einsum('a,kard->krd', onehot, model_stack.reshape(model_stack.shape[0], ADAPTERS, RANK, D), precision=lax.Precision.HIGHEST)
    hidden_rows = jnp.einsum('a,kard->krd', onehot, hidden_stack.reshape(hidden_stack.shape[0], ADAPTERS, RANK, FF), precision=lax.Precision.HIGHEST)
    proj_query = low_back(adapted(input_rows, attn_full[0], model_rows[0], model_rows[6]))
    proj_key = low_back(adapted(input_rows, attn_full[1], model_rows[1], model_rows[7]))
    proj_value = low_back(adapted(input_rows, attn_full[2], model_rows[2], model_rows[8]))
    queries = low(rotate(rms_norm(proj_query, gains_all[0]), positions))
    key_rows = low(rotate(rms_norm(proj_key, gains_all[1]), positions))
    value_rows = low(proj_value)
    mixed_out = attend(queries, key_rows, value_rows, positions, seq_length)
    attended = low(low_back(mixed_out))
    branch = low_back(adapted(attended, attn_full[3], model_rows[3], model_rows[9]))
    hidden_in = input_rows + rms_norm(branch, gains_all[2])
    hidden_low = low(hidden_in)
    gate_val = low_back(adapted(hidden_low, mlp_full[0], model_rows[4], hidden_rows[0]))
    up_val = low_back(adapted(hidden_low, mlp_full[1], model_rows[5], hidden_rows[1]))
    product = low(jax.nn.silu(gate_val) * up_val)
    feedforward_output = low_back(adapted(product, mlp_full[2].T, hidden_rows[2], model_rows[10]))
    return hidden_in + rms_norm(feedforward_output, gains_all[3])

def reference(tokens, out_grad, attn_weight, mlp_weight, norm_gains, adapt_model, adapt_hidden, lengths, adapter_pick, block_order):
    attn_full = attn_weight.astype(jnp.float32)
    mlp_full = mlp_weight.astype(jnp.float32)
    gains_all = norm_gains.astype(jnp.float32)
    model_stack = adapt_model.astype(jnp.float32)
    hidden_stack = adapt_hidden.astype(jnp.float32)

    def one_sequence(totals, seq_items):
        seq_tokens, seq_grad, seq_length, seq_pick, seq_order = seq_items
        positions = (seq_order[:, None] * BLOCK + jnp.arange(BLOCK, dtype=jnp.int32)[None, :]).reshape(-1).astype(jnp.int32)
        onehot = (jnp.arange(ADAPTERS, dtype=jnp.int32) == seq_pick).astype(jnp.float32)
        valid_rows = (positions < seq_length).astype(jnp.float32)[:, None]

        def forward(input_rows, model_part, hidden_part):
            return layer_forward(input_rows, model_part, hidden_part, onehot, attn_full, mlp_full, gains_all, positions, seq_length)
        result, pullback = jax.vjp(forward, seq_tokens.astype(jnp.float32), model_stack, hidden_stack)
        grad_inputs, grad_model, grad_hidden = pullback(seq_grad.astype(jnp.float32) * valid_rows)
        return ((totals[0] + grad_model, totals[1] + grad_hidden), (result.astype(jnp.bfloat16), grad_inputs))
    zeros_pair = (jnp.zeros(model_stack.shape, jnp.float32), jnp.zeros(hidden_stack.shape, jnp.float32))
    totals, outputs = lax.scan(one_sequence, zeros_pair, (tokens, out_grad, lengths, adapter_pick, block_order))
    return (outputs[0], outputs[1], totals[0], totals[1])
```

```python
import math

import jax
import jax.numpy as jnp
from jax import lax
from jax.sharding import PartitionSpec as P

HEADS = 16
HEAD_DIM = 128
RANK = 16
ADAPTERS = 4
NORM_EPS = 1e-06
ADAPTER_SCALE = 4.0
ROPE_BASE = 500000.0
F32 = jnp.float32
BF16 = jnp.bfloat16
CORE_SWAP = ((0, 1), (1, 0), (2, 3), (3, 2))
CHIP_SWAP = ((0, 2), (2, 0), (1, 3), (3, 1))


def dot(left, right, dims):
    return lax.dot_general(left, right, (dims, ((), ())), preferred_element_type=F32)


def mm(left, right):
    return dot(left, right, ((1,), (0,)))


def mm_t(left, right):
    return dot(left, right, ((1,), (1,)))


def tmm(left, right):
    return dot(left, right, ((0,), (0,)))


def swap_core(values):
    return lax.ppermute(values, "wsh", CORE_SWAP)


def swap_chip(values):
    return lax.ppermute(values, "wsh", CHIP_SWAP)


def sum_wsh(values):
    values = values + swap_core(values)
    return values + swap_chip(values)


def gather_wsh(block, axis, me):
    far = swap_chip(block)
    near = swap_core(block)
    far_near = swap_core(far)
    extent = block.shape[axis]
    shape = list(block.shape)
    shape[axis] = 4 * extent
    whole = jnp.zeros(shape, block.dtype)
    for flip, piece in ((0, block), (1, near), (2, far), (3, far_near)):
        start = [0] * block.ndim
        start[axis] = (me ^ flip) * extent
        whole = lax.dynamic_update_slice(whole, piece, start)
    return whole


def scatter_wsh(partial, axis, me):
    extent = partial.shape[axis] // 4

    def piece(flip):
        return lax.dynamic_slice_in_dim(partial, (me ^ flip) * extent, extent, axis)

    far = piece(2).astype(F32) + swap_core(piece(3)).astype(F32)
    far = swap_chip(far.astype(BF16))
    near = piece(0).astype(F32) + swap_core(piece(1)).astype(F32)
    return near + far.astype(F32)


def rotate(values, cosine, sine_part):
    half = HEAD_DIM // 2
    first, second = values[..., :half], values[..., half:]
    return jnp.concatenate(
        [first * cosine - second * sine_part, second * cosine + first * sine_part], axis=-1
    )


def per_device(
    tokens,
    out_grad,
    attn_weight,
    mlp_weight,
    norm_gains,
    adapt_model,
    adapt_hidden,
    lengths,
    adapter_pick,
    block_order,
):
    own_rows = tokens[0]
    rows, model_dim = own_rows.shape
    block_rows = rows // 2
    ctx_size = lax.axis_size("ctx")
    seqs = lax.axis_size("wsh")
    width = model_dim // seqs
    local_heads = width // HEAD_DIM
    me = lax.axis_index("wsh")
    ctx_index = lax.axis_index("ctx")
    pairs = seqs * local_heads
    members = math.gcd(ctx_size, pairs)
    groups = ctx_size // members
    per_member = pairs // members
    splits = local_heads // per_member
    group_rows = members * rows
    member = ctx_index % members
    group = ctx_index // members
    ctx_groups = [[g * members + i for i in range(members)] for g in range(groups)]
    key_groups = [[g * members + i for g in range(groups)] for i in range(members)]
    score_scale = HEAD_DIM ** (-0.5)
    all_rows = seqs * rows

    def columns(matrix):
        return lax.dynamic_slice_in_dim(matrix, me * width, width, 1)

    orders = gather_wsh(block_order, 0, me)
    positions = (orders[:, :, None] * block_rows + jnp.arange(block_rows)[None, None, :]).reshape(
        seqs, -1
    )
    row_positions = lax.dynamic_slice_in_dim(positions, ctx_index * rows, rows, 1)
    own_positions = lax.dynamic_index_in_dim(row_positions, me, keepdims=False)
    own_length = lax.dynamic_index_in_dim(lengths, me, keepdims=False)
    valid_rows = (own_positions < own_length).astype(F32)[:, None]
    half_dim = HEAD_DIM // 2
    frequency = ROPE_BASE ** (-(jnp.arange(half_dim, dtype=F32) * 2.0) / HEAD_DIM)
    angles = row_positions.reshape(-1).astype(F32)[:, None] * frequency[None, :]
    cosine, sine_part = jnp.cos(angles)[:, None, :], jnp.sin(angles)[:, None, :]
    picked = (jnp.arange(ADAPTERS * RANK)[None, :] // RANK == adapter_pick[:, None]).astype(F32)
    row_mask = jnp.broadcast_to(picked[:, None, :], (seqs, rows, ADAPTERS * RANK)).reshape(
        all_rows, -1
    )

    def low(product):
        return (product * row_mask).astype(BF16)

    def low_sum(partial):
        narrow = (partial * row_mask).reshape(all_rows, ADAPTERS, RANK).sum(1)
        total = jnp.tile(sum_wsh(narrow), (1, ADAPTERS))
        return (total * row_mask).astype(BF16)

    gains = norm_gains.astype(F32)
    last_gain = gather_wsh(norm_gains[3:4], 1, me).astype(F32)

    hidden = gather_wsh(own_rows, 0, me)
    rows_a = gather_wsh(jnp.concatenate([adapt_model[:6], adapt_model[10:11]], 0), 2, me)
    low_in = [low(mm_t(hidden, rows_a[k])) for k in range(3)]
    proj = [
        mm(hidden, attn_weight[k]) + ADAPTER_SCALE * mm(low_in[k], adapt_model[6 + k])
        for k in range(3)
    ]
    squares = jnp.stack([jnp.sum(proj[0] * proj[0], -1), jnp.sum(proj[1] * proj[1], -1)])
    scales = lax.rsqrt(sum_wsh(squares) / model_dim + NORM_EPS)[:, :, None]

    def heads(values):
        return values.reshape(all_rows, local_heads, HEAD_DIM)

    turned = [
        rotate(heads(proj[k] * scales[k] * gains[k]), cosine, sine_part).astype(BF16)
        for k in range(2)
    ]
    packed = jnp.stack([turned[0], turned[1], heads(proj[2].astype(BF16))])

    def to_heads(values):
        count = values.shape[0]
        shaped = values.reshape(count, seqs, rows, splits, per_member * HEAD_DIM)
        shaped = shaped.transpose(1, 3, 0, 2, 4).reshape(
            members, count, rows, per_member * HEAD_DIM
        )
        moved = lax.all_to_all(shaped, "ctx", 0, 0, tiled=True, axis_index_groups=ctx_groups)
        moved = moved.transpose(1, 0, 2, 3).reshape(count, group_rows, per_member, HEAD_DIM)
        return moved.transpose(0, 2, 1, 3)

    def to_rows(values):
        count = values.shape[0]
        shaped = values.transpose(0, 2, 1, 3).reshape(
            count, members, rows, per_member * HEAD_DIM
        )
        moved = lax.all_to_all(
            shaped.transpose(1, 0, 2, 3),
            "ctx",
            0,
            0,
            tiled=True,
            axis_index_groups=ctx_groups,
        )
        moved = moved.reshape(seqs, splits, count, rows, per_member * HEAD_DIM)
        return moved.transpose(2, 0, 3, 1, 4).reshape(count, all_rows, width)

    queries, keys, values = to_heads(packed)
    if groups > 1:
        keys, values = (
            lax.all_gather(part, "ctx", axis=1, tiled=True, axis_index_groups=key_groups)
            for part in (keys, values)
        )
    seq_here = (member * per_member) // local_heads
    key_positions = lax.dynamic_index_in_dim(positions, seq_here, keepdims=False)
    query_positions = lax.dynamic_slice_in_dim(key_positions, group * group_rows, group_rows)
    length_here = lax.dynamic_index_in_dim(lengths, seq_here, keepdims=False)
    allowed = (key_positions[None, :] <= query_positions[:, None]) & (
        key_positions[None, :] < length_here
    )

    def batched(left, right, lc, rc):
        return lax.dot_general(
            left, right, (((lc,), (rc,)), ((0,), (0,))), preferred_element_type=F32
        )

    scores = jnp.where(allowed[None], batched(queries, keys, 2, 2) * score_scale, -jnp.inf)
    row_max = jnp.max(scores, axis=-1, keepdims=True)
    log_total = row_max + jnp.log(jnp.sum(jnp.exp(scores - row_max), axis=-1, keepdims=True))
    weights = jnp.exp(scores - log_total).astype(BF16)
    attended = batched(weights, values, 2, 1).astype(BF16)
    attended = to_rows(attended[None])[0]

    attended_full = gather_wsh(attended, 1, me)
    low_out = low(mm_t(attended_full, rows_a[3]))
    branch = mm(attended_full, attn_weight[3]) + ADAPTER_SCALE * mm(low_out, adapt_model[9])
    branch_scale = lax.rsqrt(
        sum_wsh(jnp.sum(branch * branch, -1, keepdims=True)) / model_dim + NORM_EPS
    )
    mid = columns(hidden).astype(F32) + branch * branch_scale * gains[2]
    mid_low = mid.astype(BF16)
    mid_full = gather_wsh(mid_low, 1, me)

    low_gate = low(mm_t(mid_full, rows_a[4]))
    low_up = low(mm_t(mid_full, rows_a[5]))
    gate = mm(mid_full, mlp_weight[0]) + ADAPTER_SCALE * mm(low_gate, adapt_hidden[0])
    up = mm(mid_full, mlp_weight[1]) + ADAPTER_SCALE * mm(low_up, adapt_hidden[1])
    sigmoid_gate = jax.nn.sigmoid(gate)
    silu_gate = gate * sigmoid_gate
    product = (silu_gate * up).astype(BF16)
    low_down_part = mm_t(product, adapt_hidden[2])
    down_part = mm_t(product, mlp_weight[2]) + ADAPTER_SCALE * mm(low(low_down_part), rows_a[6])
    down = scatter_wsh(down_part.astype(BF16), 0, me)
    low_down = low_sum(low_down_part)
    down_scale = lax.rsqrt(jnp.mean(down * down, axis=-1, keepdims=True) + NORM_EPS)
    mid_rows = lax.dynamic_slice_in_dim(mid_full, me * rows, rows, 0).astype(F32)
    result = mid_rows + down * down_scale * last_gain

    upstream = out_grad[0].astype(F32) * valid_rows
    scaled = upstream * last_gain
    grad_down = (
        down_scale * scaled
        - down * down_scale**3 * jnp.mean(scaled * down, axis=-1, keepdims=True)
    ).astype(BF16)
    grad_down = gather_wsh(grad_down, 0, me)
    grad_low_down = low(ADAPTER_SCALE * mm_t(grad_down, rows_a[6]))
    grad_product = mm(grad_down, mlp_weight[2]) + mm(grad_low_down, adapt_hidden[2])
    grad_gate = (
        grad_product * up * sigmoid_gate * (1.0 + gate * (1.0 - sigmoid_gate))
    ).astype(BF16)
    grad_up = (grad_product * silu_gate).astype(BF16)
    low_gate_part = ADAPTER_SCALE * mm_t(grad_gate, adapt_hidden[0])
    low_up_part = ADAPTER_SCALE * mm_t(grad_up, adapt_hidden[1])
    own_block = (jnp.arange(seqs) == me).astype(F32)[:, None, None]
    mid_part = (
        mm_t(grad_gate, mlp_weight[0])
        + mm_t(grad_up, mlp_weight[1])
        + mm(low(low_gate_part), rows_a[4])
        + mm(low(low_up_part), rows_a[5])
        + (own_block * upstream[None]).reshape(all_rows, model_dim)
    )
    grad_mid = scatter_wsh(mid_part.astype(BF16), 1, me)
    grad_low_gate = low_sum(low_gate_part)
    grad_low_up = low_sum(low_up_part)
    hidden_grads = jnp.stack(
        [
            ADAPTER_SCALE * tmm(low_gate, grad_gate),
            ADAPTER_SCALE * tmm(low_up, grad_up),
            tmm(grad_low_down, product),
        ]
    )
    grad_a_gate = tmm(grad_low_gate, mid_low)
    grad_a_up = tmm(grad_low_up, mid_low)
    grad_b_down = ADAPTER_SCALE * tmm(low_down, columns(grad_down))

    scaled = grad_mid * gains[2]
    mean = sum_wsh(jnp.sum(scaled * branch, axis=-1, keepdims=True)) / model_dim
    grad_branch = (branch_scale * scaled - branch * branch_scale**3 * mean).astype(BF16)
    low_out_part = ADAPTER_SCALE * mm_t(grad_branch, adapt_model[9])
    attended_part = mm_t(grad_branch, attn_weight[3]) + mm(low(low_out_part), rows_a[3])
    grad_attended = scatter_wsh(attended_part.astype(BF16), 1, me).astype(BF16)
    grad_low_out = low_sum(low_out_part)
    grad_b_out = ADAPTER_SCALE * tmm(low_out, grad_branch)
    grad_a_out = tmm(grad_low_out, attended)

    grad_heads = to_heads(grad_attended[None])[0]
    scores = jnp.where(allowed[None], batched(queries, keys, 2, 2) * score_scale, -jnp.inf)
    weights_full = jnp.exp(scores - log_total)
    grad_probs = batched(grad_heads, values, 2, 2)
    delta = jnp.sum(weights_full * grad_probs, axis=-1, keepdims=True)
    grad_scores = (weights_full * (grad_probs - delta)).astype(BF16)
    grad_queries = batched(grad_scores, keys, 2, 1) * score_scale
    grad_keys = batched(grad_scores, queries, 1, 1) * score_scale
    grad_values = batched(weights_full.astype(BF16), grad_heads, 1, 1)
    if groups > 1:
        grad_keys, grad_values = (
            lax.psum_scatter(
                part, "ctx", scatter_dimension=1, tiled=True, axis_index_groups=key_groups
            )
            for part in (grad_keys, grad_values)
        )
    grads = to_rows(jnp.stack([grad_queries, grad_keys, grad_values]).astype(BF16))
    turned = [
        rotate(heads(grads[k].astype(F32)), cosine, -sine_part).reshape(all_rows, width) * gains[k]
        for k in range(2)
    ]
    sums = jnp.stack([jnp.sum(turned[k] * proj[k], -1) for k in range(2)])
    means = (sum_wsh(sums) / model_dim)[:, :, None]
    grad_proj = [
        (scales[k] * turned[k] - proj[k] * scales[k] ** 3 * means[k]).astype(BF16)
        for k in range(2)
    ] + [grads[2]]
    low_parts = [ADAPTER_SCALE * mm_t(grad_proj[k], adapt_model[6 + k]) for k in range(3)]
    own_column = (jnp.arange(seqs) == me).astype(F32)[None, :, None]
    input_part = (
        mm_t(grad_proj[0], attn_weight[0])
        + mm_t(grad_proj[1], attn_weight[1])
        + mm_t(grad_proj[2], attn_weight[2])
        + mm(low(low_parts[0]), rows_a[0])
        + mm(low(low_parts[1]), rows_a[1])
        + mm(low(low_parts[2]), rows_a[2])
        + (own_column * grad_mid[:, None, :]).reshape(all_rows, model_dim)
    )
    grad_inputs = scatter_wsh(input_part.astype(BF16), 0, me)
    own_hidden = columns(hidden)
    grad_a_in = [tmm(low_sum(low_parts[k]), own_hidden) for k in range(3)]
    grad_b_in = [ADAPTER_SCALE * tmm(low_in[k], grad_proj[k]) for k in range(3)]
    model_grads = jnp.stack(
        grad_a_in + [grad_a_out, grad_a_gate, grad_a_up] + grad_b_in + [grad_b_out, grad_b_down]
    )
    model_grads = lax.psum(model_grads, "ctx")
    hidden_grads = lax.psum(hidden_grads, "ctx")
    return (result.astype(BF16)[None], grad_inputs[None], model_grads, hidden_grads)


def solution(mesh):
    in_specs = (
        P("wsh", "ctx", None),
        P("wsh", "ctx", None),
        P(None, None, "wsh"),
        P(None, None, "wsh"),
        P(None, "wsh"),
        P(None, None, "wsh"),
        P(None, None, "wsh"),
        P(),
        P(),
        P("wsh", None),
    )
    out_specs = (
        P("wsh", "ctx", None),
        P("wsh", "ctx", None),
        P(None, None, "wsh"),
        P(None, None, "wsh"),
    )
    return jax.shard_map(
        per_device, mesh=mesh, in_specs=in_specs, out_specs=out_specs, check_vma=False
    )
```

```python
import math

import jax
import jax.numpy as jnp
from jax import lax
from jax.experimental import pallas as pl
from jax.experimental.pallas import tpu as pltpu
from jax.sharding import PartitionSpec as P

HEADS = 16
HEAD_DIM = 128
RANK = 16
ADAPTERS = 4
LOW = RANK * ADAPTERS
NORM_EPS = 1e-06
SCALE = 4.0
ROPE_BASE = 500000.0
MASKED = -1e30
FAR_POSITION = 1e9
F32 = jnp.float32
BF16 = jnp.bfloat16
CORE_SWAP = ((0, 1), (1, 0), (2, 3), (3, 2))
CHIP_SWAP = ((0, 2), (2, 0), (1, 3), (3, 1))


def dot(left, right, lc, rc, precision=None):
    return lax.dot_general(
        left, right, (((lc,), (rc,)), ((), ())), precision=precision, preferred_element_type=F32
    )


def mm(left, right):
    return dot(left, right, 1, 0)


def mm_t(left, right):
    return dot(left, right, 1, 1)


def tmm(left, right):
    return dot(left, right, 0, 0)


def row_sums(values, row):
    picked = lax.broadcasted_iota(jnp.int32, (8, values.shape[1]), 0) == row
    return dot(picked.astype(F32), values, 1, 1, lax.Precision.HIGHEST)


def column(block, row):
    return jnp.transpose(block)[:, row : row + 1]


def window(index, extent):
    return pl.ds(pl.multiple_of(index * extent, extent), extent)


def narrow(wide):
    return sum(wide[a * RANK : (a + 1) * RANK] for a in range(ADAPTERS))


def widen(thin, mask):
    return (jnp.concatenate([thin] * ADAPTERS, axis=0) * mask).astype(BF16)


def swap_core(values):
    return lax.ppermute(values, "wsh", CORE_SWAP)


def swap_chip(values):
    return lax.ppermute(values, "wsh", CHIP_SWAP)


def sum_wsh(values):
    values = values + swap_core(values)
    return values + swap_chip(values)


def pieces_wsh(block):
    far = swap_chip(block)
    return block, swap_core(block), far, swap_core(far)


def gather_wsh(block, axis, me):
    extent = block.shape[axis]
    shape = list(block.shape)
    shape[axis] = 4 * extent
    whole = jnp.zeros(shape, block.dtype)
    for flip, piece in enumerate(pieces_wsh(block)):
        start = [0] * block.ndim
        start[axis] = (me ^ flip) * extent
        whole = lax.dynamic_update_slice(whole, piece, start)
    return whole


def scatter_wsh(own, near, far, far_near):
    far = (far.astype(F32) + swap_core(far_near).astype(F32)).astype(BF16)
    return own, swap_core(near), swap_chip(far)


def total(refs):
    return refs[0][...].astype(F32) + refs[1][...].astype(F32) + refs[2][...].astype(F32)


def whole(array):
    rank = len(array.shape)
    return pl.BlockSpec(array.shape, lambda *_: (0,) * rank)


def kernel_call(body, name, grid, ins, outs, scratch=(), me=None, flops=0):
    arrays = [i[0] if isinstance(i, tuple) else i for i in ins]
    in_specs = [i[1] if isinstance(i, tuple) else whole(i) for i in ins]
    shapes = [o[0] if isinstance(o, tuple) else o for o in outs]
    out_specs = [o[1] if isinstance(o, tuple) else whole(o) for o in outs]
    moved = sum(math.prod(s.block_shape) * a.dtype.itemsize for s, a in zip(in_specs, arrays))
    moved += sum(math.prod(s.shape) * s.dtype.itemsize for s in shapes)
    return pl.pallas_call(
        body,
        name=name,
        out_shape=shapes,
        grid_spec=pltpu.PrefetchScalarGridSpec(
            num_scalar_prefetch=1,
            grid=grid,
            in_specs=in_specs,
            out_specs=out_specs,
            scratch_shapes=list(scratch),
        ),
        compiler_params=pltpu.CompilerParams(dimension_semantics=("arbitrary",) * len(grid)),
        cost_estimate=pl.CostEstimate(
            flops=int(flops), bytes_accessed=int(moved), transcendentals=0
        ),
    )(me, *arrays)


def shape(dims, dtype):
    return jax.ShapeDtypeStruct(dims, dtype)


def qkv_body(me, p0, p1, p2, p3, w, a, b, mask, proj, low_ref, squares, own_ref, rows_scr, low_scr):
    step = pl.program_id(0)
    rows = p0.shape[0]

    @pl.when(step == 0)
    def _():
        for flip, piece in enumerate((p0, p1, p2, p3)):
            rows_scr[window(me[0] ^ flip, rows), :] = piece[...]
        own_ref[...] = rows_scr[:, window(me[0], own_ref.shape[1])]
        squares[...] = jnp.zeros_like(squares)
        stacked = a[...].reshape(-1, a.shape[2])
        low_scr[...] = mm_t(stacked, rows_scr[...])

    low = (low_scr[pl.ds(pl.multiple_of(step * LOW, LOW), LOW), :] * mask[...]).astype(BF16)
    low_ref[0] = low
    out = mm(rows_scr[...], w[0]) + SCALE * tmm(low, b[0])
    proj[0] = out
    squares[...] += row_sums(out * out, step)


def rope_body(model_dim, per_member, me, proj, squares, gain, cosine, sine, out):
    inverse = lax.rsqrt(squares[...] * (1.0 / model_dim) + NORM_EPS)
    for k in range(3):
        scale = column(inverse, k)
        for h in range(proj.shape[2] // HEAD_DIM):
            lanes = slice(h * HEAD_DIM, (h + 1) * HEAD_DIM)
            part = proj[k, :, lanes]
            if k < 2:
                part = part * scale * gain[k : k + 1, lanes]
                part = part * cosine[...] + pltpu.roll(part, HEAD_DIM // 2, 1) * sine[...]
            spot = (h % per_member) * HEAD_DIM
            out[h // per_member, k, :, spot : spot + HEAD_DIM] = part.astype(BF16)


def probabilities(q, k, q_pos, k_pos):
    queries = q[...].reshape(-1, HEAD_DIM)
    keys = k[...].reshape(-1, HEAD_DIM)
    scores = mm_t(queries, keys) * (HEAD_DIM**-0.5)
    scores = jnp.where(k_pos[0:1, :] <= column(q_pos[...], 0), scores, MASKED)
    weights = jnp.exp(scores - jnp.max(scores, axis=-1, keepdims=True))
    return queries, keys, weights * (1.0 / jnp.sum(weights, axis=-1, keepdims=True))


def attention_body(me, q, k, v, q_pos, k_pos, out):
    _, _, weights = probabilities(q, k, q_pos, k_pos)
    mixed = mm(weights.astype(BF16), v[...].reshape(-1, HEAD_DIM))
    out[...] = mixed.astype(BF16).reshape(out.shape)


def attention_back_body(joint, me, q, k, v, g, q_pos, k_pos, *outs):
    key_scr, value_scr = outs[-2:]
    step = pl.program_id(1)
    queries, keys, weights = probabilities(q, k, q_pos, k_pos)
    grads = g[...].reshape(-1, HEAD_DIM)
    grad_probs = mm_t(grads, v[...].reshape(-1, HEAD_DIM))
    delta = jnp.sum(weights * grad_probs, axis=-1, keepdims=True)
    grad_scores = (weights * (grad_probs - delta)).astype(BF16)
    grad_queries = mm(grad_scores, keys) * (HEAD_DIM**-0.5)
    grad_keys = tmm(grad_scores, queries)
    grad_values = tmm(weights.astype(BF16), grads)
    blocks, rows = q.shape[0], q.shape[2]
    grad_queries = grad_queries.astype(BF16).reshape(blocks, rows, HEAD_DIM)
    if joint:
        outs[0][pl.ds(step * blocks, blocks), 0] = grad_queries
    else:
        outs[0][...] = grad_queries

    @pl.when(step == 0)
    def _():
        key_scr[...] = grad_keys
        value_scr[...] = grad_values

    @pl.when(step > 0)
    def _():
        key_scr[...] += grad_keys
        value_scr[...] += grad_values

    @pl.when(step == pl.num_programs(1) - 1)
    def _():
        target = outs[0] if joint else outs[1]
        first = 1 if joint else 0
        extent = (target.shape[0],) + target.shape[2:]
        target[:, first] = (key_scr[...] * (HEAD_DIM**-0.5)).astype(target.dtype).reshape(extent)
        target[:, first + 1] = value_scr[...].astype(target.dtype).reshape(extent)


def branch_body(me, p0, p1, p2, p3, w, a, b, mask, branch, low_ref, squares):
    out = None
    low = None
    splits, rows, extent = p0.shape[1:]
    for flip, piece in enumerate((p0, p1, p2, p3)):
        for part in range(splits):
            at = window((me[0] ^ flip) * splits + part, extent)
            left = piece[:, part].reshape(-1, extent)
            term = mm(left, w[0, at, :])
            low_term = mm_t(a[0, :, at], left)
            out = term if out is None else out + term
            low = low_term if low is None else low + low_term
    low = (low * mask[...]).astype(BF16)
    low_ref[...] = low
    out = out + SCALE * tmm(low, b[0])
    branch[...] = out
    squares[...] = row_sums(out * out, 0)


def mid_body(model_dim, me, own, branch, squares, gain, out):
    scale = lax.rsqrt(column(squares[...], 0) * (1.0 / model_dim) + NORM_EPS)
    out[...] = (own[...].astype(F32) + branch[...] * scale * gain[2:3, :]).astype(BF16)


def mlp_body(
    me, p0, p1, p2, p3, wg, wu, wd, a, bg, bu, ad, b_down, mask,
    gate_ref, up_ref, product_ref, low_ref, low_down, mid_rows, o0, o1, o2, o3,
    rows_scr, low_scr, acc,
):
    step = pl.program_id(0)
    width = p0.shape[1]

    @pl.when(step == 0)
    def _():
        for flip, piece in enumerate((p0, p1, p2, p3)):
            rows_scr[:, window(me[0] ^ flip, width)] = piece[...]
        mid_rows[...] = rows_scr[window(me[0], mid_rows.shape[0]), :]
        stacked = mm_t(a[...].reshape(-1, a.shape[2]), rows_scr[...])
        for k in range(2):
            low_ref[k] = (stacked[k * LOW : (k + 1) * LOW] * mask[...]).astype(BF16)
        low_scr[...] = jnp.zeros_like(low_scr)

    gate = mm(rows_scr[...], wg[0]) + SCALE * tmm(low_ref[0], bg[0])
    up = mm(rows_scr[...], wu[0]) + SCALE * tmm(low_ref[1], bu[0])
    gate_ref[...] = gate
    up_ref[...] = up
    product = (gate * jax.nn.sigmoid(gate) * up).astype(BF16)
    product_ref[...] = product
    low_scr[...] += mm_t(ad[0], product)
    part = mm_t(product, wd[0])

    @pl.when(step == 0)
    def _():
        acc[...] = part

    @pl.when(step > 0)
    def _():
        acc[...] += part

    @pl.when(step == pl.num_programs(0) - 1)
    def _():
        low = low_scr[...] * mask[...]
        low_down[...] = narrow(low)
        acc[...] += SCALE * tmm(low.astype(BF16), b_down[0])
        for flip, out in enumerate((o0, o1, o2, o3)):
            out[...] = acc[window(me[0] ^ flip, out.shape[0]), :].astype(BF16)


def turn_body(me, y0, y1, y2, mid_rows, upstream_ref, valid, gain, result, grad, masked):
    down = total((y0, y1, y2))
    scale = lax.rsqrt(jnp.mean(down * down, axis=-1, keepdims=True) + NORM_EPS)
    result[...] = (mid_rows[...].astype(F32) + down * scale * gain[0:1, :]).astype(BF16)
    upstream = upstream_ref[0].astype(F32) * column(valid[...], 0)
    masked[...] = upstream.astype(BF16)
    scaled = upstream * gain[0:1, :]
    mean = jnp.mean(scaled * down, axis=-1, keepdims=True)
    grad[...] = (scale * scaled - down * (scale * scale * scale) * mean).astype(BF16)


def mlp_back_body(
    me, p0, p1, p2, p3, masked, wg, wu, wd, a, bg, bu, ad, b_down, mask,
    gate_ref, up_ref, product_ref, low_ref, low_down,
    grads, grad_b_down, low_parts, o0, o1, o2, o3,
    rows_scr, low_scr, part_scr, acc,
):
    step = pl.program_id(0)
    rows = p0.shape[0]
    width = o0.shape[1]

    @pl.when(step == 0)
    def _():
        for flip, piece in enumerate((p0, p1, p2, p3)):
            rows_scr[window(me[0] ^ flip, rows), :] = piece[...]
        low_scr[...] = (SCALE * mm_t(b_down[0], rows_scr[...]) * mask[...]).astype(BF16)
        wide = widen(low_down[...], mask[...])
        grad_b_down[...] = SCALE * mm(wide, rows_scr[:, window(me[0], width)])
        part_scr[...] = jnp.zeros_like(part_scr)
        acc[...] = jnp.zeros_like(acc)
        acc[window(me[0], rows), :] = masked[...].astype(F32)

    grad_product = mm(rows_scr[...], wd[0]) + tmm(low_scr[...], ad[0])
    gate = gate_ref[...]
    sigmoid = jax.nn.sigmoid(gate)
    silu = gate * sigmoid
    grad_up = (grad_product * silu).astype(BF16)
    grad_gate = (
        grad_product * up_ref[...] * sigmoid * (1.0 + gate * (1.0 - sigmoid))
    ).astype(BF16)
    grads[0] = SCALE * mm(low_ref[0], grad_gate)
    grads[1] = SCALE * mm(low_ref[1], grad_up)
    grads[2] = mm(low_scr[...], product_ref[...])
    part_scr[0] += SCALE * mm_t(bg[0], grad_gate)
    part_scr[1] += SCALE * mm_t(bu[0], grad_up)
    acc[...] += mm_t(grad_gate, wg[0]) + mm_t(grad_up, wu[0])

    @pl.when(step == pl.num_programs(0) - 1)
    def _():
        for k in range(2):
            low = part_scr[k] * mask[...]
            low_parts[k] = narrow(low)
            acc[...] += tmm(low.astype(BF16), a[k])
        for flip, out in enumerate((o0, o1, o2, o3)):
            out[...] = acc[:, window(me[0] ^ flip, width)].astype(BF16)


def mid_sum_body(me, y0, y1, y2, branch, gain, grad_mid, sums):
    grad = total((y0, y1, y2))
    grad_mid[...] = grad
    sums[...] = row_sums(grad * gain[2:3, :] * branch[...], 0)


def branch_back_body(
    model_dim, me, grad_mid, branch, squares, sums, gain, w, a, b, mask, low_out, low_sums, mid,
    grad_b, grad_a, low_parts, o0, o1, o2, o3,
):
    scale = lax.rsqrt(column(squares[...], 0) * (1.0 / model_dim) + NORM_EPS)
    mean = column(sums[...], 0) * (1.0 / model_dim)
    scaled = grad_mid[...] * gain[2:3, :]
    grad = (scale * scaled - branch[...] * (scale * scale * scale) * mean).astype(BF16)
    low = SCALE * mm_t(b[0], grad) * mask[...]
    low_parts[...] = narrow(low)
    low = low.astype(BF16)
    width = o0.shape[1]
    for flip, out in enumerate((o0, o1, o2, o3)):
        at = window(me[0] ^ flip, width)
        out[...] = (mm_t(grad, w[0, at, :]) + tmm(low, a[0, :, at])).astype(BF16)
    grad_b[...] = SCALE * mm(low_out[...], grad)
    for k in range(2):
        grad_a[k] = mm(widen(low_sums[k], mask[...]), mid[...])


def heads_body(y0, y1, y2):
    return total((y0, y1, y2))


def split_body(per_member, me, y0, y1, y2, out):
    grad = total((y0, y1, y2)).astype(BF16)
    extent = per_member * HEAD_DIM
    for part in range(out.shape[0]):
        out[part] = grad[:, part * extent : (part + 1) * extent]


def turn_back_body(per_member, me, grads, proj, gain, cosine, sine, turned, sums):
    result = None
    for k in range(3):
        dots = None
        for h in range(proj.shape[2] // HEAD_DIM):
            lanes = slice(h * HEAD_DIM, (h + 1) * HEAD_DIM)
            spot = (h % per_member) * HEAD_DIM
            part = grads[h // per_member, k, :, spot : spot + HEAD_DIM].astype(F32)
            if k < 2:
                part = part * cosine[...] - pltpu.roll(part, HEAD_DIM // 2, 1) * sine[...]
                part = part * gain[k : k + 1, lanes]
                term = row_sums(part * proj[k, :, lanes], k)
                result = term if result is None else result + term
            turned[k, :, lanes] = part
    sums[...] = result


def qkv_back_body(
    model_dim, me, turned, proj, squares, sums, grad_mid, w, a, b, mask, low_ref,
    grad_b, low_parts, o0, o1, o2, o3, acc,
):
    step = pl.program_id(0)

    @pl.when(step == 0)
    def _():
        acc[...] = jnp.zeros_like(acc)
        acc[:, window(me[0], grad_mid.shape[1])] = grad_mid[...]

    here = lax.broadcasted_iota(jnp.int32, squares.shape, 0) == step

    def chosen(values):
        row = jnp.sum(jnp.where(here, values, 0.0), axis=0, keepdims=True)
        return column(jnp.broadcast_to(row, values.shape), 0)

    scale = chosen(lax.rsqrt(squares[...] * (1.0 / model_dim) + NORM_EPS))
    mean = chosen(sums[...]) * (1.0 / model_dim)
    scale = jnp.where(step == 2, 1.0, scale)
    mean = jnp.where(step == 2, 0.0, mean)
    grad = (scale * turned[0] - proj[0] * (scale * scale * scale) * mean).astype(BF16)
    low = SCALE * mm_t(b[0], grad) * mask[...]
    low_parts[0] = narrow(low)
    grad_b[0] = SCALE * mm(low_ref[0], grad)
    acc[...] += mm_t(grad, w[0]) + tmm(low.astype(BF16), a[0])

    @pl.when(step == pl.num_programs(0) - 1)
    def _():
        for flip, out in enumerate((o0, o1, o2, o3)):
            out[...] = acc[window(me[0] ^ flip, out.shape[0]), :].astype(BF16)


def last_grads_body(me, low_in, low_out, own, attended, mask, grad_in, grad_out):
    for k in range(3):
        grad_in[k] = mm(widen(low_in[k], mask[...]), own[...])
    wide = widen(low_out[...], mask[...])
    splits, rows, extent = attended.shape[1:]
    for part in range(splits):
        grad_out[:, part * extent : (part + 1) * extent] = mm(
            wide, attended[:, part].reshape(-1, extent)
        )


def per_device(
    tokens,
    out_grad,
    attn_weight,
    mlp_weight,
    norm_gains,
    adapt_model,
    adapt_hidden,
    lengths,
    adapter_pick,
    block_order,
):
    own_rows = tokens[0]
    rows, model_dim = own_rows.shape
    block_rows = rows // 2
    ctx_size = lax.axis_size("ctx")
    seqs = lax.axis_size("wsh")
    width = model_dim // seqs
    hidden_width = mlp_weight.shape[2]
    local_heads = width // HEAD_DIM
    me = lax.axis_index("wsh")
    here = me.astype(jnp.int32).reshape(1)
    ctx_index = lax.axis_index("ctx")
    pairs = seqs * local_heads
    members = math.gcd(ctx_size, pairs)
    groups = ctx_size // members
    per_member = pairs // members
    splits = local_heads // per_member
    span = per_member * HEAD_DIM
    group_rows = members * rows
    member = ctx_index % members
    group = ctx_index // members
    ctx_groups = [[g * members + i for i in range(members)] for g in range(groups)]
    key_groups = [[g * members + i for g in range(groups)] for i in range(members)]
    all_rows = seqs * rows

    def call(body, name, grid, ins, outs, scratch=(), flops=0):
        return kernel_call(body, name, grid, ins, outs, scratch, here, flops)

    def bind(body, *fixed):
        def bound(*refs):
            return body(*fixed, *refs)

        return bound

    orders = gather_wsh(block_order, 0, me)
    positions = (orders[:, :, None] * block_rows + jnp.arange(block_rows)[None, None, :]).reshape(
        seqs, -1
    )
    row_positions = lax.dynamic_slice_in_dim(positions, ctx_index * rows, rows, 1)
    own_positions = lax.dynamic_index_in_dim(row_positions, me, keepdims=False)
    own_length = lax.dynamic_index_in_dim(lengths, me, keepdims=False)
    valid = jnp.broadcast_to((own_positions < own_length).astype(F32)[None], (8, rows))
    half = HEAD_DIM // 2
    frequency = ROPE_BASE ** (-(jnp.arange(half, dtype=F32) * 2.0) / HEAD_DIM)
    angles = row_positions.reshape(-1).astype(F32)[:, None] * frequency[None, :]
    cosine, sine = jnp.cos(angles), jnp.sin(angles)
    cosine = jnp.concatenate([cosine, cosine], 1)
    sine = jnp.concatenate([-sine, sine], 1)
    picked = jnp.arange(LOW)[:, None] // RANK == adapter_pick[None, :]
    mask = jnp.repeat(picked.astype(F32), rows, axis=1)
    seq_here = (member * per_member) // local_heads
    key_positions = lax.dynamic_index_in_dim(positions, seq_here, keepdims=False)
    query_positions = lax.dynamic_slice_in_dim(key_positions, group * group_rows, group_rows)
    length_here = lax.dynamic_index_in_dim(lengths, seq_here, keepdims=False)
    key_positions = jnp.where(
        key_positions < length_here, key_positions.astype(F32), FAR_POSITION
    )
    k_pos = jnp.broadcast_to(key_positions[None], (8, key_positions.shape[0]))
    q_pos = jnp.broadcast_to(query_positions.astype(F32)[None], (8, group_rows))
    gains = norm_gains.astype(F32)

    hidden = pieces_wsh(own_rows)
    rows_a = gather_wsh(jnp.concatenate([adapt_model[:6], adapt_model[10:11]], 0), 2, me)
    last_gain = jnp.broadcast_to(
        gather_wsh(norm_gains[3:4], 1, me).astype(F32), (8, model_dim)
    )

    def stack_block(index):
        return pl.BlockSpec((1, all_rows, width), lambda k, *_: (k, 0, 0))

    w_qkv = (attn_weight, pl.BlockSpec((1, model_dim, width), lambda k, *_: (k, 0, 0)))
    w_out = (attn_weight, pl.BlockSpec((1, model_dim, width), lambda *_: (3, 0, 0)))
    a_qkv = (rows_a, pl.BlockSpec((3, LOW, model_dim), lambda *_: (0, 0, 0)))
    a_step = (rows_a, pl.BlockSpec((1, LOW, model_dim), lambda k, *_: (k, 0, 0)))
    a_out = (rows_a, pl.BlockSpec((1, LOW, model_dim), lambda *_: (3, 0, 0)))
    a_mlp = (rows_a, pl.BlockSpec((2, LOW, model_dim), lambda *_: (2, 0, 0)))
    b_down = (rows_a, pl.BlockSpec((1, LOW, model_dim), lambda *_: (6, 0, 0)))
    b_step = (adapt_model, pl.BlockSpec((1, LOW, width), lambda k, *_: (6 + k, 0, 0)))
    b_out = (adapt_model, pl.BlockSpec((1, LOW, width), lambda *_: (9, 0, 0)))
    step_rows = pl.BlockSpec((1, all_rows, width), lambda k, *_: (k, 0, 0))
    step_low = pl.BlockSpec((1, LOW, all_rows), lambda k, *_: (k, 0, 0))

    matmul = 2.0 * all_rows * model_dim * width

    proj, low_in, squares, own_columns = call(
        qkv_body,
        "qkv",
        (3,),
        [*hidden, w_qkv, a_qkv, b_step, mask],
        [
            (shape((3, all_rows, width), F32), step_rows),
            (shape((3, LOW, all_rows), BF16), step_low),
            shape((8, all_rows), F32),
            shape((all_rows, width), BF16),
        ],
        [pltpu.VMEM((all_rows, model_dim), BF16), pltpu.VMEM((3 * LOW, all_rows), F32)],
        3 * matmul,
    )
    squares = sum_wsh(squares)
    proj_rows = (proj, pl.BlockSpec((3, rows, width), lambda s, *_: (0, s, 0)))
    tables = [(t, pl.BlockSpec((rows, HEAD_DIM), lambda s, *_: (s, 0))) for t in (cosine, sine)]
    lane_rows = pl.BlockSpec((8, rows), lambda s, *_: (0, s))
    member_rows = pl.BlockSpec((splits, 3, rows, span), lambda s, *_: (s, 0, 0, 0))
    (packed,) = call(
        bind(rope_body, model_dim, per_member),
        "rope",
        (seqs,),
        [proj_rows, (squares, lane_rows), gains, *tables],
        [(shape((members, 3, rows, span), BF16), member_rows)],
    )

    def exchange(values):
        return lax.all_to_all(values, "ctx", 0, 0, tiled=True, axis_index_groups=ctx_groups)

    heads = exchange(packed)
    if groups > 1:
        keyed = lax.all_gather(
            heads[:, 1:], "ctx", axis=0, tiled=True, axis_index_groups=key_groups
        )
        first = 0
    else:
        keyed, first = heads, 1
    key_blocks = keyed.shape[0]
    query_blocks = 2
    query_rows = query_blocks * rows
    attention_ins = [
        (heads, pl.BlockSpec((query_blocks, 1, rows, HEAD_DIM), lambda p, i, *_: (i, 0, 0, p))),
        (keyed, pl.BlockSpec((key_blocks, 1, rows, HEAD_DIM), lambda p, i, *_: (0, first, 0, p))),
        (
            keyed,
            pl.BlockSpec((key_blocks, 1, rows, HEAD_DIM), lambda p, i, *_: (0, first + 1, 0, p)),
        ),
    ]
    position_ins = [(q_pos, pl.BlockSpec((8, query_rows), lambda p, i, *_: (0, i))), k_pos]
    row_block = pl.BlockSpec((query_blocks, rows, HEAD_DIM), lambda p, i, *_: (i, 0, p))
    attention_grid = (per_member, members // query_blocks)
    score_flops = 2.0 * per_member * group_rows * key_blocks * rows * HEAD_DIM
    (attended,) = call(
        attention_body,
        "attention",
        attention_grid,
        attention_ins + position_ins,
        [(shape((members, rows, span), BF16), row_block)],
        flops=2 * score_flops,
    )
    attended = exchange(attended).reshape(seqs, splits, rows, span)

    attended_pieces = pieces_wsh(attended)
    branch, low_out, branch_squares = call(
        branch_body,
        "branch",
        (1,),
        [*attended_pieces, w_out, a_out, b_out, mask],
        [shape((all_rows, width), F32), shape((LOW, all_rows), BF16), shape((8, all_rows), F32)],
        flops=matmul,
    )
    branch_squares = sum_wsh(branch_squares)
    (mid,) = call(
        bind(mid_body, model_dim),
        "mid",
        (1,),
        [own_columns, branch, branch_squares, gains],
        [shape((all_rows, width), BF16)],
    )

    tile = 256
    steps = hidden_width // tile

    def w_mlp(index):
        return (mlp_weight, pl.BlockSpec((1, model_dim, tile), lambda j, *_: (index, 0, j)))

    def hidden_low(index):
        return (adapt_hidden, pl.BlockSpec((1, LOW, tile), lambda j, *_: (index, 0, j)))

    tile_rows = pl.BlockSpec((all_rows, tile), lambda j, *_: (0, j))
    mid_pieces = pieces_wsh(mid)
    weights = [w_mlp(0), w_mlp(1), w_mlp(2), a_mlp]
    weights += [hidden_low(0), hidden_low(1), hidden_low(2), b_down, mask]
    wide = shape((all_rows, hidden_width), F32)
    gate, up, product, low_mid, low_down, mid_rows, *parts = call(
        mlp_body,
        "mlp",
        (steps,),
        [*mid_pieces, *weights],
        [
            (wide, tile_rows),
            (wide, tile_rows),
            (shape((all_rows, hidden_width), BF16), tile_rows),
            shape((2, LOW, all_rows), BF16),
            shape((RANK, all_rows), F32),
            shape((rows, model_dim), BF16),
        ]
        + [shape((rows, model_dim), BF16)] * 4,
        [
            pltpu.VMEM((all_rows, model_dim), BF16),
            pltpu.VMEM((LOW, all_rows), F32),
            pltpu.VMEM((all_rows, model_dim), F32),
        ],
        12 * matmul,
    )
    down_parts = scatter_wsh(*parts)
    low_down = sum_wsh(low_down)
    result, grad_down, masked = call(
        turn_body,
        "turn",
        (1,),
        [*down_parts, mid_rows, out_grad, valid, last_gain],
        [shape((rows, model_dim), BF16)] * 3,
    )

    grad_pieces = pieces_wsh(grad_down)
    hidden_grads, grad_b_down, low_parts, *parts = call(
        mlp_back_body,
        "mlp_back",
        (steps,),
        [*grad_pieces, masked, *weights]
        + [(gate, tile_rows), (up, tile_rows), (product, tile_rows), low_mid, low_down],
        [
            (shape((3, LOW, hidden_width), F32), pl.BlockSpec((3, LOW, tile), lambda j, *_: (0, 0, j))),
            shape((LOW, width), F32),
            shape((2, RANK, all_rows), F32),
        ]
        + [shape((all_rows, width), BF16)] * 4,
        [
            pltpu.VMEM((all_rows, model_dim), BF16),
            pltpu.VMEM((LOW, all_rows), BF16),
            pltpu.VMEM((2, LOW, all_rows), F32),
            pltpu.VMEM((all_rows, model_dim), F32),
        ],
        12 * matmul,
    )
    mid_parts = scatter_wsh(*parts)
    low_parts = sum_wsh(low_parts)

    grad_mid, mid_sums = call(
        mid_sum_body,
        "mid_sum",
        (1,),
        [*mid_parts, branch, gains],
        [shape((all_rows, width), F32), shape((8, all_rows), F32)],
    )
    mid_sums = sum_wsh(mid_sums)
    grad_b_out, grad_a_mid, low_out_parts, *parts = call(
        bind(branch_back_body, model_dim),
        "branch_back",
        (1,),
        [grad_mid, branch, branch_squares, mid_sums, gains, w_out, a_out, b_out, mask]
        + [low_out, low_parts, mid],
        [
            shape((LOW, width), F32),
            shape((2, LOW, width), F32),
            shape((RANK, all_rows), F32),
        ]
        + [shape((all_rows, width), BF16)] * 4,
        flops=matmul,
    )
    early_grads = jnp.stack([grad_a_mid[0], grad_a_mid[1], grad_b_out, grad_b_down])
    early_grads, hidden_grads = lax.psum((early_grads, hidden_grads), "ctx")
    low_out_parts = sum_wsh(low_out_parts)
    attended_parts = scatter_wsh(*parts)
    seq_rows = pl.BlockSpec((rows, width), lambda s, *_: (s, 0))
    (grad_attended,) = call(
        bind(split_body, per_member),
        "split",
        (seqs,),
        [(part, seq_rows) for part in attended_parts],
        [(shape((members, rows, span), BF16), pl.BlockSpec((splits, rows, span), lambda s, *_: (s, 0, 0)))],
    )

    grad_heads = exchange(grad_attended)
    back_ins = attention_ins + [(grad_heads, row_block)] + position_ins
    key_scratch = [pltpu.VMEM((key_blocks * rows, HEAD_DIM), F32)] * 2
    if groups == 1:
        (grads,) = call(
            bind(attention_back_body, True),
            "attention_back",
            attention_grid,
            back_ins,
            [
                (
                    shape((members, 3, rows, span), BF16),
                    pl.BlockSpec((members, 3, rows, HEAD_DIM), lambda p, i, *_: (0, 0, 0, p)),
                )
            ],
            key_scratch,
            5 * score_flops,
        )
    else:
        grad_queries, grad_keyed = call(
            bind(attention_back_body, False),
            "attention_back",
            attention_grid,
            back_ins,
            [
                (shape((members, rows, span), BF16), row_block),
                (
                    shape((key_blocks, 2, rows, span), F32),
                    pl.BlockSpec((key_blocks, 2, rows, HEAD_DIM), lambda p, i, *_: (0, 0, 0, p)),
                ),
            ],
            key_scratch,
            5 * score_flops,
        )
        grad_keyed = lax.psum_scatter(
            grad_keyed, "ctx", scatter_dimension=0, tiled=True, axis_index_groups=key_groups
        )
        grads = jnp.concatenate([grad_queries[:, None], grad_keyed.astype(BF16)], 1)
    grads = exchange(grads)
    turned, sums = call(
        bind(turn_back_body, per_member),
        "turn_back",
        (seqs,),
        [(grads, member_rows), proj_rows, gains, *tables],
        [
            (shape((3, all_rows, width), F32), pl.BlockSpec((3, rows, width), lambda s, *_: (0, s, 0))),
            (shape((8, all_rows), F32), lane_rows),
        ],
    )
    sums = sum_wsh(sums)
    grad_b_in, low_in_parts, *parts = call(
        bind(qkv_back_body, model_dim),
        "qkv_back",
        (3,),
        [(turned, step_rows), (proj, step_rows), squares, sums, grad_mid]
        + [w_qkv, a_step, b_step, mask, (low_in, step_low)],
        [
            (shape((3, LOW, width), F32), pl.BlockSpec((1, LOW, width), lambda k, *_: (k, 0, 0))),
            (shape((3, RANK, all_rows), F32), pl.BlockSpec((1, RANK, all_rows), lambda k, *_: (k, 0, 0))),
        ]
        + [shape((rows, model_dim), BF16)] * 4,
        [pltpu.VMEM((all_rows, model_dim), F32)],
        3 * matmul,
    )
    low_in_parts = sum_wsh(low_in_parts)
    input_parts = scatter_wsh(*parts)
    grad_inputs = sum(part.astype(F32) for part in input_parts)
    grad_a_in, grad_a_out = call(
        last_grads_body,
        "last_grads",
        (1,),
        [low_in_parts, low_out_parts, own_columns, attended, mask],
        [shape((3, LOW, width), F32), shape((LOW, width), F32)],
    )
    late = jnp.concatenate([grad_a_in, grad_a_out[None], grad_b_in], 0).astype(BF16)
    count = late.shape[0]
    late = late.reshape(ctx_size, -1, width)
    late = lax.all_to_all(late, "ctx", 0, 0, tiled=True).astype(F32).sum(0).astype(BF16)
    late = jnp.broadcast_to(late[None], (ctx_size,) + late.shape)
    late = lax.all_to_all(late, "ctx", 0, 0, tiled=True).astype(F32).reshape(count, LOW, width)
    model_grads = jnp.concatenate(
        [late[:4], early_grads[:2], late[4:7], early_grads[2:]], 0
    )
    return (result[None], grad_inputs[None], model_grads, hidden_grads)


def solution(mesh):
    in_specs = (
        P("wsh", "ctx", None),
        P("wsh", "ctx", None),
        P(None, None, "wsh"),
        P(None, None, "wsh"),
        P(None, "wsh"),
        P(None, None, "wsh"),
        P(None, None, "wsh"),
        P(),
        P(),
        P("wsh", None),
    )
    out_specs = (
        P("wsh", "ctx", None),
        P("wsh", "ctx", None),
        P(None, None, "wsh"),
        P(None, None, "wsh"),
    )
    return jax.shard_map(
        per_device, mesh=mesh, in_specs=in_specs, out_specs=out_specs, check_vma=False
    )
```

```python
import math

import jax
import jax.numpy as jnp
from jax import lax
from jax.experimental import pallas as pl
from jax.experimental.pallas import tpu as pltpu
from jax.sharding import PartitionSpec as P

HEADS = 16
HEAD_DIM = 128
RANK = 16
ADAPTERS = 4
LOW = RANK * ADAPTERS
NORM_EPS = 1e-06
SCALE = 4.0
ROPE_BASE = 500000.0
MASKED = -1e30
FAR_POSITION = 1e9
F32 = jnp.float32
BF16 = jnp.bfloat16
CORE_SWAP = ((0, 1), (1, 0), (2, 3), (3, 2))
CHIP_SWAP = ((0, 2), (2, 0), (1, 3), (3, 1))


def dot(left, right, lc, rc, precision=None):
    return lax.dot_general(
        left, right, (((lc,), (rc,)), ((), ())), precision=precision, preferred_element_type=F32
    )


def mm(left, right):
    return dot(left, right, 1, 0)


def mm_t(left, right):
    return dot(left, right, 1, 1)


def tmm(left, right):
    return dot(left, right, 0, 0)


def row_sums(values, row):
    picked = lax.broadcasted_iota(jnp.int32, (8, values.shape[1]), 0) == row
    return dot(picked.astype(F32), values, 1, 1, lax.Precision.HIGHEST)


def column(block, row):
    return jnp.transpose(block)[:, row : row + 1]


def window(index, extent):
    return pl.ds(pl.multiple_of(index * extent, extent), extent)


def narrow(wide):
    return sum(wide[a * RANK : (a + 1) * RANK] for a in range(ADAPTERS))


def widen(thin, mask):
    return (jnp.concatenate([thin] * ADAPTERS, axis=0) * mask).astype(BF16)


def swap_core(values):
    return lax.ppermute(values, "wsh", CORE_SWAP)


def swap_chip(values):
    return lax.ppermute(values, "wsh", CHIP_SWAP)


def sum_wsh(values):
    values = values + swap_core(values)
    return values + swap_chip(values)


def pieces_wsh(block):
    far = swap_chip(block)
    return block, swap_core(block), far, swap_core(far)


def gather_wsh(block, axis, me):
    extent = block.shape[axis]
    shape = list(block.shape)
    shape[axis] = 4 * extent
    whole = jnp.zeros(shape, block.dtype)
    for flip, piece in enumerate(pieces_wsh(block)):
        start = [0] * block.ndim
        start[axis] = (me ^ flip) * extent
        whole = lax.dynamic_update_slice(whole, piece, start)
    return whole


def scatter_wsh(own, near, far, far_near):
    far = (far.astype(F32) + swap_core(far_near).astype(F32)).astype(BF16)
    return own, swap_core(near), swap_chip(far)


def total(refs):
    return refs[0][...].astype(F32) + refs[1][...].astype(F32) + refs[2][...].astype(F32)


def whole(array):
    rank = len(array.shape)
    return pl.BlockSpec(array.shape, lambda *_: (0,) * rank)


def kernel_call(body, name, grid, ins, outs, scratch, me, flops, keep, after, grant):
    arrays = [i[0] if isinstance(i, tuple) else i for i in ins]
    in_specs = [i[1] if isinstance(i, tuple) else whole(i) for i in ins]
    shapes = [o[0] if isinstance(o, tuple) else o for o in outs]
    out_specs = [o[1] if isinstance(o, tuple) else whole(o) for o in outs]
    moved = sum(math.prod(s.block_shape) * a.dtype.itemsize for s, a in zip(in_specs, arrays))
    moved += sum(math.prod(s.block_shape) * a.dtype.itemsize for s, a in zip(out_specs, shapes))
    first = 1 + len(arrays)
    extra = [array for array, _ in keep] + list(after)

    def run(*refs):
        return body(*refs[:first], *refs[first + len(extra) :])

    return pl.pallas_call(
        run,
        name=name,
        out_shape=shapes,
        grid_spec=pltpu.PrefetchScalarGridSpec(
            num_scalar_prefetch=1,
            grid=grid,
            in_specs=in_specs + [pl.BlockSpec(memory_space=pl.ANY)] * len(extra),
            out_specs=out_specs,
            scratch_shapes=list(scratch),
        ),
        input_output_aliases={first + i: out for i, (_, out) in enumerate(keep)},
        compiler_params=pltpu.CompilerParams(
            dimension_semantics=("arbitrary",) * len(grid), vmem_limit_bytes=grant << 20
        ),
        cost_estimate=pl.CostEstimate(
            flops=int(flops), bytes_accessed=int(moved * math.prod(grid)), transcendentals=0
        ),
    )(me, *arrays, *extra)


def shape(dims, dtype):
    return jax.ShapeDtypeStruct(dims, dtype)


def qkv_body(me, p0, p1, w, a, b, mask, proj, low_ref, squares, own_ref, rows_scr, low_scr):
    step = pl.program_id(0)
    rows = p0.shape[0]

    @pl.when(step == 0)
    def _():
        rows_scr[window(me[1], rows), :] = p0[...]
        rows_scr[window(1 - me[1], rows), :] = p1[...]
        own_ref[...] = rows_scr[:, window(me[0], own_ref.shape[1])]
        squares[...] = jnp.zeros_like(squares)
        stacked = a[...].reshape(-1, a.shape[2])
        low_scr[...] = mm_t(stacked, rows_scr[...])

    low = (low_scr[pl.ds(pl.multiple_of(step * LOW, LOW), LOW), :] * mask[...]).astype(BF16)
    low_ref[0] = low
    out = mm(rows_scr[...], w[0]) + SCALE * tmm(low, b[0])
    proj[0] = out
    squares[...] += row_sums(out * out, step)


def rope_body(model_dim, per_member, me, proj, squares, gain, cosine, sine, out):
    inverse = lax.rsqrt(squares[...] * (1.0 / model_dim) + NORM_EPS)
    for k in range(3):
        scale = column(inverse, k)
        for h in range(proj.shape[2] // HEAD_DIM):
            lanes = slice(h * HEAD_DIM, (h + 1) * HEAD_DIM)
            part = proj[k, :, lanes]
            if k < 2:
                part = part * scale * gain[k : k + 1, lanes]
                part = part * cosine[...] + pltpu.roll(part, HEAD_DIM // 2, 1) * sine[...]
            spot = (h % per_member) * HEAD_DIM
            out[h // per_member, k, :, spot : spot + HEAD_DIM] = part.astype(BF16)


def probabilities(q, k, q_pos, k_pos):
    queries = q[...].reshape(-1, HEAD_DIM)
    keys = k[...].reshape(-1, HEAD_DIM)
    scores = mm_t(queries, keys) * (HEAD_DIM**-0.5)
    scores = jnp.where(k_pos[0:1, :] <= column(q_pos[...], 0), scores, MASKED)
    weights = jnp.exp(scores - jnp.max(scores, axis=-1, keepdims=True))
    return queries, keys, weights * (1.0 / jnp.sum(weights, axis=-1, keepdims=True))


def attention_body(me, q, k, v, q_pos, k_pos, out):
    _, _, weights = probabilities(q, k, q_pos, k_pos)
    mixed = mm(weights.astype(BF16), v[...].reshape(-1, HEAD_DIM))
    out[...] = mixed.astype(BF16).reshape(out.shape)


def attention_back_body(joint, me, q, k, v, g, q_pos, k_pos, *outs):
    key_scr, value_scr = outs[-2:]
    step = pl.program_id(1)
    queries, keys, weights = probabilities(q, k, q_pos, k_pos)
    grads = g[...].reshape(-1, HEAD_DIM)
    grad_probs = mm_t(grads, v[...].reshape(-1, HEAD_DIM))
    delta = jnp.sum(weights * grad_probs, axis=-1, keepdims=True)
    grad_scores = (weights * (grad_probs - delta)).astype(BF16)
    grad_queries = mm(grad_scores, keys) * (HEAD_DIM**-0.5)
    grad_keys = tmm(grad_scores, queries)
    grad_values = tmm(weights.astype(BF16), grads)
    blocks, rows = q.shape[0], q.shape[2]
    grad_queries = grad_queries.astype(BF16).reshape(blocks, rows, HEAD_DIM)
    if joint:
        outs[0][pl.ds(step * blocks, blocks), 0] = grad_queries
    else:
        outs[0][...] = grad_queries

    @pl.when(step == 0)
    def _():
        key_scr[...] = grad_keys
        value_scr[...] = grad_values

    @pl.when(step > 0)
    def _():
        key_scr[...] += grad_keys
        value_scr[...] += grad_values

    @pl.when(step == pl.num_programs(1) - 1)
    def _():
        target = outs[0] if joint else outs[1]
        first = 1 if joint else 0
        extent = (target.shape[0],) + target.shape[2:]
        target[:, first] = (key_scr[...] * (HEAD_DIM**-0.5)).astype(target.dtype).reshape(extent)
        target[:, first + 1] = value_scr[...].astype(target.dtype).reshape(extent)


def branch_body(me, p0, p1, p2, p3, w, a, b, mask, branch, low_ref, squares):
    out = None
    low = None
    splits, rows, extent = p0.shape[1:]
    for flip, piece in enumerate((p0, p1, p2, p3)):
        for part in range(splits):
            at = window((me[0] ^ flip) * splits + part, extent)
            left = piece[:, part].reshape(-1, extent)
            term = mm(left, w[0, at, :])
            low_term = mm_t(a[0, :, at], left)
            out = term if out is None else out + term
            low = low_term if low is None else low + low_term
    low = (low * mask[...]).astype(BF16)
    low_ref[...] = low
    out = out + SCALE * tmm(low, b[0])
    branch[...] = out
    squares[...] = row_sums(out * out, 0)


def mid_body(model_dim, me, own, branch, squares, gain, out):
    scale = lax.rsqrt(column(squares[...], 0) * (1.0 / model_dim) + NORM_EPS)
    out[...] = (own[...].astype(F32) + branch[...] * scale * gain[2:3, :]).astype(BF16)


def mlp_body(
    near, me, p0, p1, p2, p3, wg, wu, wd, a, bg, bu, ad, b_down, mask, *refs
):
    gate_ref, up_ref, product_ref, low_ref, low_down, *refs = refs
    rows_scr, low_scr, acc = refs[-3:]
    parts = refs[:2]
    step = pl.program_id(0)
    width = p0.shape[1]

    @pl.when(step == 0)
    def _():
        for flip, piece in enumerate((p0, p1, p2, p3)):
            rows_scr[:, window(me[0] ^ flip, width)] = piece[...]
        if near:
            mid_rows = refs[2]
            mid_rows[...] = rows_scr[window(me[1], mid_rows.shape[0]), :]
        stacked = mm_t(a[...].reshape(-1, a.shape[2]), rows_scr[...])
        for k in range(2):
            low_ref[k] = (stacked[k * LOW : (k + 1) * LOW] * mask[...]).astype(BF16)
        low_scr[...] = jnp.zeros_like(low_scr)
        acc[...] = jnp.zeros_like(acc)

    gate = mm(rows_scr[...], wg[0]) + SCALE * tmm(low_ref[0], bg[0])
    up = mm(rows_scr[...], wu[0]) + SCALE * tmm(low_ref[1], bu[0])
    gate_ref[...] = gate
    up_ref[...] = up
    product = (gate * jax.nn.sigmoid(gate) * up).astype(BF16)
    product_ref[...] = product
    low_scr[...] += mm_t(ad[0], product)
    acc[...] += mm_t(product, wd[0])

    @pl.when(step == pl.num_programs(0) - 1)
    def _():
        low = low_scr[...] * mask[...]
        low_down[...] = narrow(low)
        acc[...] += SCALE * tmm(low.astype(BF16), b_down[0])
        for flip, out in enumerate(parts):
            out[...] = acc[window(me[1] ^ flip, out.shape[0]), :].astype(BF16)


def turn_body(me, y0, y1, y2, mid_rows, upstream_ref, valid, gain, result, grad, masked):
    down = total((y0, y1, y2))
    scale = lax.rsqrt(jnp.mean(down * down, axis=-1, keepdims=True) + NORM_EPS)
    result[...] = (mid_rows[...].astype(F32) + down * scale * gain[0:1, :]).astype(BF16)
    upstream = upstream_ref[0].astype(F32) * column(valid[...], 0)
    masked[...] = upstream.astype(BF16)
    scaled = upstream * gain[0:1, :]
    mean = jnp.mean(scaled * down, axis=-1, keepdims=True)
    grad[...] = (scale * scaled - down * (scale * scale * scale) * mean).astype(BF16)


def mlp_back_body(
    near, me, p0, p1, seed, wg, wu, wd, a, bg, bu, ad, b_down, mask,
    gate_ref, up_ref, product_ref, low_ref,
    grads, own_ref, low_parts, o0, o1, o2, o3,
    rows_scr, low_scr, part_scr, acc,
):
    step = pl.program_id(0)
    rows = p0.shape[0]
    width = o0.shape[1]

    @pl.when(step == 0)
    def _():
        rows_scr[window(me[1], rows), :] = p0[...]
        rows_scr[window(1 - me[1], rows), :] = p1[...]
        own_ref[...] = rows_scr[:, window(me[0], width)]
        low_scr[...] = (SCALE * mm_t(b_down[0], rows_scr[...]) * mask[...]).astype(BF16)
        part_scr[...] = jnp.zeros_like(part_scr)
        acc[...] = jnp.zeros_like(acc)
        if near:
            acc[window(me[1], rows), :] = seed[...].astype(F32)

    grad_product = mm(rows_scr[...], wd[0]) + tmm(low_scr[...], ad[0])
    gate = gate_ref[...]
    sigmoid = jax.nn.sigmoid(gate)
    silu = gate * sigmoid
    grad_up = (grad_product * silu).astype(BF16)
    grad_gate = (
        grad_product * up_ref[...] * sigmoid * (1.0 + gate * (1.0 - sigmoid))
    ).astype(BF16)
    terms = (
        SCALE * mm(low_ref[0], grad_gate),
        SCALE * mm(low_ref[1], grad_up),
        mm(low_scr[...], product_ref[...]),
    )
    for k, term in enumerate(terms):
        grads[k] = term if near else term + seed[k]
    part_scr[0] += SCALE * mm_t(bg[0], grad_gate)
    part_scr[1] += SCALE * mm_t(bu[0], grad_up)
    acc[...] += mm_t(grad_gate, wg[0]) + mm_t(grad_up, wu[0])

    @pl.when(step == pl.num_programs(0) - 1)
    def _():
        for k in range(2):
            low = part_scr[k] * mask[...]
            low_parts[k] = narrow(low)
            acc[...] += tmm(low.astype(BF16), a[k])
        for flip, out in enumerate((o0, o1, o2, o3)):
            out[...] = acc[:, window(me[0] ^ flip, width)].astype(BF16)


def mid_sum_body(me, y0, y1, y2, z0, z1, z2, branch, gain, grad_mid, sums):
    half = y0.shape[0]
    chip = me[0] // 2
    grad_mid[window(chip, half), :] = total((y0, y1, y2))
    grad_mid[window(1 - chip, half), :] = total((z0, z1, z2))
    sums[...] = row_sums(grad_mid[...] * gain[2:3, :] * branch[...], 0)


def branch_back_body(
    model_dim, me, grad_mid, branch, squares, sums, gain, w, a, b, mask, low_out, low_sums, mid,
    low_down, grad_down, grads, low_parts, o0, o1, o2, o3,
):
    scale = lax.rsqrt(column(squares[...], 0) * (1.0 / model_dim) + NORM_EPS)
    mean = column(sums[...], 0) * (1.0 / model_dim)
    scaled = grad_mid[...] * gain[2:3, :]
    grad = (scale * scaled - branch[...] * (scale * scale * scale) * mean).astype(BF16)
    low = SCALE * mm_t(b[0], grad) * mask[...]
    low_parts[...] = narrow(low)
    low = low.astype(BF16)
    width = grad.shape[1]
    seqs, splits, rows, span = o0.shape
    for flip, out in enumerate((o0, o1, o2, o3)):
        at = window(me[0] ^ flip, width)
        part = (mm_t(grad, w[0, at, :]) + tmm(low, a[0, :, at])).astype(BF16)
        for i in range(splits):
            out[:, i] = part[:, i * span : (i + 1) * span].reshape(seqs, rows, span)
    for k in range(2):
        grads[k] = mm(widen(low_sums[k], mask[...]), mid[...]).astype(BF16)
    grads[2] = (SCALE * mm(low_out[...], grad)).astype(BF16)
    grads[3] = (SCALE * mm(widen(low_down[...], mask[...]), grad_down[...])).astype(BF16)


def turn_back_body(per_member, me, grads, proj, gain, cosine, sine, turned, sums):
    result = None
    for k in range(3):
        dots = None
        for h in range(proj.shape[2] // HEAD_DIM):
            lanes = slice(h * HEAD_DIM, (h + 1) * HEAD_DIM)
            spot = (h % per_member) * HEAD_DIM
            part = grads[h // per_member, k, :, spot : spot + HEAD_DIM].astype(F32)
            if k < 2:
                part = part * cosine[...] - pltpu.roll(part, HEAD_DIM // 2, 1) * sine[...]
                part = part * gain[k : k + 1, lanes]
                term = row_sums(part * proj[k, :, lanes], k)
                result = term if result is None else result + term
            turned[k, :, lanes] = part
    sums[...] = result


def qkv_grad_body(
    model_dim, me, turned, proj, squares, sums, b, mask, low_ref, grad_ref, grad_b, low_wide, low_parts
):
    step = pl.program_id(0)
    here = lax.broadcasted_iota(jnp.int32, squares.shape, 0) == step

    def chosen(values):
        row = jnp.sum(jnp.where(here, values, 0.0), axis=0, keepdims=True)
        return column(jnp.broadcast_to(row, values.shape), 0)

    scale = chosen(lax.rsqrt(squares[...] * (1.0 / model_dim) + NORM_EPS))
    mean = chosen(sums[...]) * (1.0 / model_dim)
    scale = jnp.where(step == 2, 1.0, scale)
    mean = jnp.where(step == 2, 0.0, mean)
    grad = (scale * turned[0] - proj[0] * (scale * scale * scale) * mean).astype(BF16)
    grad_ref[0] = grad
    low = SCALE * mm_t(b[0], grad) * mask[...]
    low_parts[0] = narrow(low)
    low_wide[0] = low.astype(BF16)
    grad_b[0] = (SCALE * mm(low_ref[0], grad)).astype(BF16)


def qkv_back_body(me, grad, low, grad_mid, w, a, o0, o1, acc):
    step = pl.program_id(0)

    @pl.when(step == 0)
    def _():
        acc[...] = jnp.zeros_like(acc)
        acc[:, window(me[0], grad_mid.shape[1])] = grad_mid[...]

    acc[...] += mm_t(grad[0], w[0]) + tmm(low[0], a[0])

    @pl.when(step == pl.num_programs(0) - 1)
    def _():
        for flip, out in enumerate((o0, o1)):
            out[...] = acc[window(me[1] ^ flip, out.shape[0]), :].astype(BF16)


def last_grads_body(me, low_in, low_out, own, attended, mask, grads):
    for k in range(3):
        grads[k] = mm(widen(low_in[k], mask[...]), own[...]).astype(BF16)
    wide = widen(low_out[...], mask[...])
    splits, rows, extent = attended.shape[1:]
    for part in range(splits):
        grads[3, :, part * extent : (part + 1) * extent] = mm(
            wide, attended[:, part].reshape(-1, extent)
        ).astype(BF16)


def per_device(
    tokens,
    out_grad,
    attn_weight,
    mlp_weight,
    norm_gains,
    adapt_model,
    adapt_hidden,
    lengths,
    adapter_pick,
    block_order,
):
    own_rows = tokens[0]
    rows, model_dim = own_rows.shape
    block_rows = rows // 2
    ctx_size = lax.axis_size("ctx")
    seqs = lax.axis_size("wsh")
    width = model_dim // seqs
    hidden_width = mlp_weight.shape[2]
    local_heads = width // HEAD_DIM
    me = lax.axis_index("wsh")
    here = jnp.stack([me, me % 2, me // 2]).astype(jnp.int32)
    ctx_index = lax.axis_index("ctx")
    pairs = seqs * local_heads
    members = math.gcd(ctx_size, pairs)
    groups = ctx_size // members
    per_member = pairs // members
    splits = local_heads // per_member
    span = per_member * HEAD_DIM
    group_rows = members * rows
    member = ctx_index % members
    group = ctx_index // members
    ctx_groups = [[g * members + i for i in range(members)] for g in range(groups)]
    key_groups = [[g * members + i for g in range(groups)] for i in range(members)]
    all_rows = seqs * rows

    def call(body, name, grid, ins, outs, scratch=(), flops=0, keep=(), after=(), grant=40):
        return kernel_call(
            body, name, grid, ins, outs, scratch, here, flops, keep, after, grant
        )

    def bind(body, *fixed):
        def bound(*refs):
            return body(*fixed, *refs)

        return bound

    rows_qkv = gather_wsh(adapt_model[:3], 2, me)
    hidden = pieces_wsh(own_rows)
    rest = lax.optimization_barrier(
        (jnp.concatenate([adapt_model[3:6], adapt_model[10:11]], 0), norm_gains, hidden[2])
    )
    rows_a = gather_wsh(rest[0], 2, me)
    last_gain = jnp.broadcast_to(gather_wsh(rest[1][3:4], 1, me).astype(F32), (8, model_dim))

    orders = gather_wsh(block_order, 0, me)
    positions = (orders[:, :, None] * block_rows + jnp.arange(block_rows)[None, None, :]).reshape(
        seqs, -1
    )
    row_positions = lax.dynamic_slice_in_dim(positions, ctx_index * rows, rows, 1)
    own_positions = lax.dynamic_index_in_dim(row_positions, me, keepdims=False)
    own_length = lax.dynamic_index_in_dim(lengths, me, keepdims=False)
    valid = jnp.broadcast_to((own_positions < own_length).astype(F32)[None], (8, rows))
    half = HEAD_DIM // 2
    frequency = ROPE_BASE ** (-(jnp.arange(half, dtype=F32) * 2.0) / HEAD_DIM)
    angles = row_positions.reshape(-1).astype(F32)[:, None] * frequency[None, :]
    cosine, sine = jnp.cos(angles), jnp.sin(angles)
    cosine = jnp.concatenate([cosine, cosine], 1)
    sine = jnp.concatenate([-sine, sine], 1)
    picked = jnp.arange(LOW)[:, None] // RANK == adapter_pick[None, :]
    mask = jnp.repeat(picked.astype(F32), rows, axis=1)
    seq_here = (member * per_member) // local_heads
    key_positions = lax.dynamic_index_in_dim(positions, seq_here, keepdims=False)
    query_positions = lax.dynamic_slice_in_dim(key_positions, group * group_rows, group_rows)
    length_here = lax.dynamic_index_in_dim(lengths, seq_here, keepdims=False)
    key_positions = jnp.where(
        key_positions < length_here, key_positions.astype(F32), FAR_POSITION
    )
    k_pos = jnp.broadcast_to(key_positions[None], (8, key_positions.shape[0]))
    q_pos = jnp.broadcast_to(query_positions.astype(F32)[None], (8, group_rows))
    gains = norm_gains.astype(F32)

    w_qkv = (attn_weight, pl.BlockSpec((1, model_dim, width), lambda k, *_: (k, 0, 0)))
    w_out = (attn_weight, pl.BlockSpec((1, model_dim, width), lambda *_: (3, 0, 0)))
    a_qkv = (rows_qkv, pl.BlockSpec((3, LOW, model_dim), lambda *_: (0, 0, 0)))
    a_step = (rows_qkv, pl.BlockSpec((1, LOW, model_dim), lambda k, *_: (k, 0, 0)))
    a_out = (rows_a, pl.BlockSpec((1, LOW, model_dim), lambda *_: (0, 0, 0)))
    a_gate = (rows_a, pl.BlockSpec((1, LOW, model_dim), lambda *_: (1, 0, 0)))
    a_up = (rows_a, pl.BlockSpec((1, LOW, model_dim), lambda *_: (2, 0, 0)))
    b_down = (rows_a, pl.BlockSpec((1, LOW, model_dim), lambda *_: (3, 0, 0)))
    b_step = (adapt_model, pl.BlockSpec((1, LOW, width), lambda k, *_: (6 + k, 0, 0)))
    b_out = (adapt_model, pl.BlockSpec((1, LOW, width), lambda *_: (9, 0, 0)))
    step_rows = pl.BlockSpec((1, all_rows, width), lambda k, *_: (k, 0, 0))
    step_low = pl.BlockSpec((1, LOW, all_rows), lambda k, *_: (k, 0, 0))

    matmul = 2.0 * all_rows * model_dim * width

    pair_rows = 2 * rows

    def half_rows(side, dims):
        def block(*args):
            half = args[-1][2] ^ side
            return tuple(half if d == -1 else (args[d] if d < 9 else 0) for d in dims)

        return block

    NONE = 9

    state = ()
    for side, pieces in ((0, hidden[:2]), (1, hidden[2:])):
        state = call(
            qkv_body,
            "qkv",
            (3,),
            [*pieces, w_qkv, a_qkv, b_step]
            + [(mask, pl.BlockSpec((LOW, pair_rows), half_rows(side, (NONE, -1))))],
            [
                (
                    shape((3, all_rows, width), F32),
                    pl.BlockSpec((1, pair_rows, width), half_rows(side, (0, -1, NONE))),
                ),
                (
                    shape((3, LOW, all_rows), BF16),
                    pl.BlockSpec((1, LOW, pair_rows), half_rows(side, (0, NONE, -1))),
                ),
                (shape((8, all_rows), F32), pl.BlockSpec((8, pair_rows), half_rows(side, (NONE, -1)))),
                (
                    shape((all_rows, width), BF16),
                    pl.BlockSpec((pair_rows, width), half_rows(side, (-1, NONE))),
                ),
            ],
            [pltpu.VMEM((pair_rows, model_dim), BF16), pltpu.VMEM((3 * LOW, pair_rows), F32)],
            1.5 * matmul,
            keep=[(array, i) for i, array in enumerate(state)],
        )
    proj, low_in, squares, own_columns = state
    squares = sum_wsh(squares)
    proj_rows = (proj, pl.BlockSpec((3, rows, width), lambda s, *_: (0, s, 0)))
    tables = [(t, pl.BlockSpec((rows, HEAD_DIM), lambda s, *_: (s, 0))) for t in (cosine, sine)]
    lane_rows = pl.BlockSpec((8, rows), lambda s, *_: (0, s))
    member_rows = pl.BlockSpec((splits, 3, rows, span), lambda s, *_: (s, 0, 0, 0))
    (packed,) = call(
        bind(rope_body, model_dim, per_member),
        "rope",
        (seqs,),
        [proj_rows, (squares, lane_rows), gains, *tables],
        [(shape((members, 3, rows, span), BF16), member_rows)],
    )

    def exchange(values):
        return lax.all_to_all(values, "ctx", 0, 0, tiled=True, axis_index_groups=ctx_groups)

    heads = exchange(packed)
    if groups > 1:
        keyed = lax.all_gather(
            heads[:, 1:], "ctx", axis=0, tiled=True, axis_index_groups=key_groups
        )
        first = 0
    else:
        keyed, first = heads, 1
    key_blocks = keyed.shape[0]
    query_blocks = 2
    query_rows = query_blocks * rows
    attention_ins = [
        (heads, pl.BlockSpec((query_blocks, 1, rows, HEAD_DIM), lambda p, i, *_: (i, 0, 0, p))),
        (keyed, pl.BlockSpec((key_blocks, 1, rows, HEAD_DIM), lambda p, i, *_: (0, first, 0, p))),
        (
            keyed,
            pl.BlockSpec((key_blocks, 1, rows, HEAD_DIM), lambda p, i, *_: (0, first + 1, 0, p)),
        ),
    ]
    position_ins = [(q_pos, pl.BlockSpec((8, query_rows), lambda p, i, *_: (0, i))), k_pos]
    row_block = pl.BlockSpec((query_blocks, rows, HEAD_DIM), lambda p, i, *_: (i, 0, p))
    attention_grid = (per_member, members // query_blocks)
    score_flops = 2.0 * per_member * group_rows * key_blocks * rows * HEAD_DIM
    (attended,) = call(
        attention_body,
        "attention",
        attention_grid,
        attention_ins + position_ins,
        [(shape((members, rows, span), BF16), row_block)],
        flops=2 * score_flops,
    )
    attended = exchange(attended).reshape(seqs, splits, rows, span)

    attended_pieces = pieces_wsh(attended)
    branch, low_out, branch_squares = call(
        branch_body,
        "branch",
        (1,),
        [*attended_pieces, w_out, a_out, b_out, mask],
        [shape((all_rows, width), F32), shape((LOW, all_rows), BF16), shape((8, all_rows), F32)],
        flops=matmul,
    )
    branch_squares = sum_wsh(branch_squares)
    (mid,) = call(
        bind(mid_body, model_dim),
        "mid",
        (1,),
        [own_columns, branch, branch_squares, gains],
        [shape((all_rows, width), BF16)],
    )

    tile = 512
    steps = hidden_width // tile

    def w_mlp(index):
        return (mlp_weight, pl.BlockSpec((1, model_dim, tile), lambda j, *_: (index, 0, j)))

    def hidden_low(index):
        return (adapt_hidden, pl.BlockSpec((1, LOW, tile), lambda j, *_: (index, 0, j)))

    def side_weights(side):
        return [w_mlp(0), w_mlp(1), w_mlp(2), a_pair, hidden_low(0), hidden_low(1)] + [
            hidden_low(2),
            b_down,
            (mask, pl.BlockSpec((LOW, pair_rows), half_rows(side, (NONE, -1)))),
        ]

    a_pair = (rows_a[1:3], pl.BlockSpec((2, LOW, model_dim), lambda *_: (0, 0, 0)))
    mid_pieces = pieces_wsh(mid)
    state = ()
    parts = {}
    for side in (1, 0):
        tile_rows = pl.BlockSpec((pair_rows, tile), half_rows(side, (-1, 0)))
        rows_here = pl.BlockSpec((pair_rows, width), half_rows(side, (-1, NONE)))
        result = call(
            bind(mlp_body, side == 0),
            "mlp",
            (steps,),
            [(piece, rows_here) for piece in mid_pieces] + side_weights(side),
            [
                (shape((all_rows, hidden_width), F32), tile_rows),
                (shape((all_rows, hidden_width), F32), tile_rows),
                (shape((all_rows, hidden_width), BF16), tile_rows),
                (
                    shape((2, LOW, all_rows), BF16),
                    pl.BlockSpec((2, LOW, pair_rows), half_rows(side, (NONE, NONE, -1))),
                ),
                (
                    shape((RANK, all_rows), F32),
                    pl.BlockSpec((RANK, pair_rows), half_rows(side, (NONE, -1))),
                ),
            ]
            + [shape((rows, model_dim), BF16)] * (3 - side),
            [
                pltpu.VMEM((pair_rows, model_dim), BF16),
                pltpu.VMEM((LOW, pair_rows), F32),
                pltpu.VMEM((pair_rows, model_dim), F32),
            ],
            6 * matmul,
            keep=[(array, i) for i, array in enumerate(state)],
        )
        state, parts[side] = result[:5], result[5:]
    gate, up, product, low_mid, low_down = state
    far = (parts[1][0].astype(F32) + swap_core(parts[1][1]).astype(F32)).astype(BF16)
    mid_rows = parts[0][2]
    result_rows, grad_down, masked = call(
        turn_body,
        "turn",
        (1,),
        [parts[0][0], swap_core(parts[0][1]), swap_chip(far), mid_rows, out_grad, valid, last_gain],
        [shape((rows, model_dim), BF16)] * 3,
        grant=20,
    )

    grad_pieces = pieces_wsh(grad_down)
    state = ()
    seed = masked
    parts = {}
    for side, pieces in ((0, grad_pieces[:2]), (1, grad_pieces[2:])):
        tile_rows = pl.BlockSpec((pair_rows, tile), half_rows(side, (-1, 0)))
        step_grads = pl.BlockSpec((3, LOW, tile), lambda j, *_: (0, 0, j))
        hidden_grads, *result = call(
            bind(mlp_back_body, side == 0),
            "mlp_back",
            (steps,),
            [*pieces, seed if side == 0 else (seed, step_grads), *side_weights(side)]
            + [(gate, tile_rows), (up, tile_rows), (product, tile_rows)]
            + [(low_mid, pl.BlockSpec((2, LOW, pair_rows), half_rows(side, (NONE, NONE, -1))))],
            [
                (shape((3, LOW, hidden_width), F32), step_grads),
                (
                    shape((all_rows, width), BF16),
                    pl.BlockSpec((pair_rows, width), half_rows(side, (-1, NONE))),
                ),
                (
                    shape((2, RANK, all_rows), F32),
                    pl.BlockSpec((2, RANK, pair_rows), half_rows(side, (NONE, NONE, -1))),
                ),
            ]
            + [shape((pair_rows, width), BF16)] * 4,
            [
                pltpu.VMEM((pair_rows, model_dim), BF16),
                pltpu.VMEM((LOW, pair_rows), BF16),
                pltpu.VMEM((2, LOW, pair_rows), F32),
                pltpu.VMEM((pair_rows, model_dim), F32),
            ],
            6 * matmul,
            keep=[(array, i + 1) for i, array in enumerate(state)],
        )
        seed, state, parts[side] = hidden_grads, result[:2], scatter_wsh(*result[2:])
    grad_down_own, low_parts = state

    def sum_ctx(values):
        count, lanes = values.shape
        values = values.astype(BF16).reshape(ctx_size, -1, lanes)
        values = lax.all_to_all(values, "ctx", 0, 0, tiled=True).astype(F32).sum(0).astype(BF16)
        values = jnp.broadcast_to(values[None], (ctx_size,) + values.shape)
        values = lax.all_to_all(values, "ctx", 0, 0, tiled=True)
        return values.astype(F32).reshape(count, lanes)

    hidden_grads = sum_ctx(hidden_grads.reshape(3 * LOW, hidden_width)).reshape(
        3, LOW, hidden_width
    )
    low_down = sum_wsh(low_down)
    low_parts = sum_wsh(low_parts)

    near, far = parts[0], parts[1]
    grad_mid, mid_sums = call(
        mid_sum_body,
        "mid_sum",
        (1,),
        [near[0], near[1], far[2], far[0], far[1], near[2], branch, gains],
        [shape((all_rows, width), F32), shape((8, all_rows), F32)],
        grant=20,
    )
    mid_sums = sum_wsh(mid_sums)
    pieces_shape = shape((seqs, splits, rows, span), BF16)
    early_grads, low_out_parts, *parts = call(
        bind(branch_back_body, model_dim),
        "branch_back",
        (1,),
        [grad_mid, branch, branch_squares, mid_sums, gains, w_out, a_out, b_out, mask]
        + [low_out, low_parts, mid, low_down, grad_down_own],
        [shape((4, LOW, width), BF16), shape((RANK, all_rows), F32)] + [pieces_shape] * 4,
        flops=matmul,
    )
    low_out_parts = sum_wsh(low_out_parts)
    attended_parts = scatter_wsh(*parts)
    grad_attended = sum(part.astype(F32) for part in attended_parts).astype(BF16)
    grad_attended = grad_attended.reshape(members, rows, span)

    grad_heads = exchange(grad_attended)
    back_ins = attention_ins + [(grad_heads, row_block)] + position_ins
    key_scratch = [pltpu.VMEM((key_blocks * rows, HEAD_DIM), F32)] * 2
    if groups == 1:
        (grads,) = call(
            bind(attention_back_body, True),
            "attention_back",
            attention_grid,
            back_ins,
            [
                (
                    shape((members, 3, rows, span), BF16),
                    pl.BlockSpec((members, 3, rows, HEAD_DIM), lambda p, i, *_: (0, 0, 0, p)),
                )
            ],
            key_scratch,
            5 * score_flops,
        )
    else:
        grad_queries, grad_keyed = call(
            bind(attention_back_body, False),
            "attention_back",
            attention_grid,
            back_ins,
            [
                (shape((members, rows, span), BF16), row_block),
                (
                    shape((key_blocks, 2, rows, span), F32),
                    pl.BlockSpec((key_blocks, 2, rows, HEAD_DIM), lambda p, i, *_: (0, 0, 0, p)),
                ),
            ],
            key_scratch,
            5 * score_flops,
        )
        grad_keyed = lax.psum_scatter(
            grad_keyed, "ctx", scatter_dimension=0, tiled=True, axis_index_groups=key_groups
        )
        grads = jnp.concatenate([grad_queries[:, None], grad_keyed.astype(BF16)], 1)
    grads = exchange(grads)
    turned, sums = call(
        bind(turn_back_body, per_member),
        "turn_back",
        (seqs,),
        [(grads, member_rows), proj_rows, gains, *tables],
        [
            (shape((3, all_rows, width), F32), pl.BlockSpec((3, rows, width), lambda s, *_: (0, s, 0))),
            (shape((8, all_rows), F32), lane_rows),
        ],
    )
    sums = sum_wsh(sums)
    half_low = pl.BlockSpec((1, LOW, width), lambda k, *_: (k, 0, 0))
    grad_proj, grad_b_in, low_wide, low_in_parts = call(
        bind(qkv_grad_body, model_dim),
        "qkv_grad",
        (3,),
        [(turned, step_rows), (proj, step_rows), squares, sums, b_step, mask, (low_in, step_low)],
        [
            (shape((3, all_rows, width), BF16), step_rows),
            (shape((3, LOW, width), BF16), half_low),
            (shape((3, LOW, all_rows), BF16), step_low),
            (
                shape((3, RANK, all_rows), F32),
                pl.BlockSpec((1, RANK, all_rows), lambda k, *_: (k, 0, 0)),
            ),
        ],
        grant=20,
    )

    def input_grads(side, after):
        return call(
            qkv_back_body,
            "qkv_back",
            (3,),
            [
                (grad_proj, pl.BlockSpec((1, pair_rows, width), half_rows(side, (0, -1, NONE)))),
                (low_wide, pl.BlockSpec((1, LOW, pair_rows), half_rows(side, (0, NONE, -1)))),
                (grad_mid, pl.BlockSpec((pair_rows, width), half_rows(side, (-1, NONE)))),
                w_qkv,
                a_step,
            ],
            [shape((rows, model_dim), BF16)] * 2,
            [pltpu.VMEM((pair_rows, model_dim), F32)],
            1.5 * matmul,
            after=after,
        )

    far_parts = input_grads(1, ())
    low_in_parts = sum_wsh(low_in_parts)
    (last_grads,) = call(
        last_grads_body,
        "last_grads",
        (1,),
        [low_in_parts, low_out_parts, own_columns, attended, mask],
        [shape((4, LOW, width), BF16)],
        after=far_parts[:1],
        grant=20,
    )
    near_parts = input_grads(0, (last_grads,))
    input_parts = scatter_wsh(*near_parts, *far_parts)
    grad_inputs = sum(part.astype(F32) for part in input_parts)
    model_grads = jnp.concatenate(
        [last_grads, early_grads[:2], grad_b_in, early_grads[2:]], 0
    )
    model_grads = sum_ctx(model_grads.reshape(-1, width)).reshape(-1, LOW, width)
    return (result_rows[None], grad_inputs[None], model_grads, hidden_grads)


def solution(mesh):
    in_specs = (
        P("wsh", "ctx", None),
        P("wsh", "ctx", None),
        P(None, None, "wsh"),
        P(None, None, "wsh"),
        P(None, "wsh"),
        P(None, None, "wsh"),
        P(None, None, "wsh"),
        P(),
        P(),
        P("wsh", None),
    )
    out_specs = (
        P("wsh", "ctx", None),
        P("wsh", "ctx", None),
        P(None, None, "wsh"),
        P(None, None, "wsh"),
    )
    return jax.shard_map(
        per_device, mesh=mesh, in_specs=in_specs, out_specs=out_specs, check_vma=False
    )
```
